32 devices in a mesh: dp: 4 (over x, core), ctx: 8 (over z, y).
Axes of the slice: x: 2, y: 2, z: 4, core: 2. Of those that a mesh axis runs over, the one named last changes fastest.
Arguments:
- hidden_in: bfloat16 [4, 1024, 960], P('dp', 'ctx'), may hold values from -6 to 6
- positions: int32 [4, 1024], P('dp', 'ctx'), may hold values from 0 to 1023, as said below
- attn_gain: bfloat16 [960], P('ctx'), may hold values from 0.099609375 to 1.8984375
- query_w: bfloat16 [960, 960], P('ctx', 'dp'), may hold values from -0.1875 to 0.1875
- key_w: bfloat16 [960, 320], P('ctx', 'dp'), may hold values from -0.1875 to 0.1875
- value_weight: bfloat16 [960, 320], P('ctx', 'dp'), may hold values from -0.1875 to 0.1875
- output_weight: bfloat16 [960, 960], P('ctx', 'dp'), may hold values from -3.5 to 3.5
- ffn_gain: bfloat16 [960], P('ctx'), may hold values from 0.099609375 to 1.8984375
- gate_w: bfloat16 [960, 2560], P('ctx', 'dp'), may hold values from -0.1875 to 0.1875
- up_w: bfloat16 [960, 2560], P('ctx', 'dp'), may hold values from -0.1875 to 0.1875
- down_w: bfloat16 [2560, 960], P('ctx', 'dp'), may hold values from -0.125 to 0.125
- cotangent: bfloat16 [4, 1024, 960], P('dp', 'ctx'), may hold values from -6 to 6
Outputs:
- hidden_out: float32 [4, 1024, 960], P('dp', 'ctx')
- grad_in: float32 [4, 1024, 960], P('dp', 'ctx')
- grad_attn_gain: float32 [960], P('ctx')
- grad_query: float32 [960, 960], P('ctx', 'dp')
- grad_key: float32 [960, 320], P('ctx', 'dp')
- grad_value: float32 [960, 320], P('ctx', 'dp')
- grad_out: float32 [960, 960], P('ctx', 'dp')
- grad_ffn_gain: float32 [960], P('ctx')
- grad_gate: float32 [960, 2560], P('ctx', 'dp')
- grad_up: float32 [960, 2560], P('ctx', 'dp')
- grad_down: float32 [2560, 960], P('ctx', 'dp')
The draws below stay inside these ranges and needn't reach their ends.
Inputs may be any that keep to these rules, and one draw needn't show every extreme that they name: In each sequence every position 0 to 1023 appears once. The 128 tokens of ctx shard c of a sequence are two aligned blocks: positions j * 64 onward and then (15 - j) * 64 onward, for a pair number j that is a permutation of the shards, drawn afresh for each sequence.
All inputs are finite; a program needn't handle non-finite values.
Results may differ from the reference program's by a relative error of at most 0.014.
Values may be sent and summed in bfloat16 or wider, within the bound.
No kernel may reach another device: no remote copies, remote signals or barrier semaphores. Data moves between devices by JAX's collectives and lax.ppermute only.
A program may use at most 192 MiB of HBM per device.

```python
import jax
import jax.numpy as jnp
from jax import lax

EMBED_WIDTH = 960
QUERY_HEADS = 15
KEY_VALUE_HEADS = 5
HEAD_SIZE = 64
FF = 2560
BLK = 64
PAIRS = 8
SEQ_LEN = 1024
SEQS = 4


def pair_order(seed_key):
    return jax.random.permutation(seed_key, PAIRS)


def draw_positions(key, part):
    seed_keys = jax.random.split(key, SEQS)
    orders = jax.vmap(pair_order)(seed_keys).astype(jnp.int32)
    within = jnp.arange(BLK, dtype=jnp.int32)
    low_block = orders[:, :, None] * BLK + within[None, None, :]
    high_block = (2 * PAIRS - 1 - orders)[:, :, None] * BLK + within[None, None, :]
    return jnp.concatenate([low_block, high_block], axis=2).reshape(SEQS, SEQ_LEN).astype(jnp.int32)


def block_levels(stream_key, extent, pieces, low, largest):
    gain, own = 1.0, jax.random.fold_in(stream_key, 6)
    for dim, parts in pieces:
        steps = jnp.exp(jax.random.uniform(jax.random.fold_in(own, dim), (parts,), jnp.float32, low / len(pieces), largest / len(pieces)))
        gain = gain * jnp.repeat(steps, extent[dim] // parts).reshape([-1 if axis == dim else 1 for axis in range(len(extent))])
    return gain


def scatter_about(key, shape, spread, reach, shards=(), held_as=jnp.bfloat16):
    result = spread * jax.random.normal(key, shape, jnp.float32)
    if shards:
        result = result * block_levels(key, shape, shards, -0.22, 0.18)
    return jnp.clip(result, -reach, reach).astype(held_as)


def setup_inputs(seed: int = 0) -> dict:
    seeds = jax.random.split(jax.random.key(seed), 13)
    return {
        "hidden_in": scatter_about(seeds[0], (SEQS, SEQ_LEN, EMBED_WIDTH), 1.0, 6.0, ((0, 4), (1, 8))),
        "positions": draw_positions(jax.random.fold_in(seeds[12], 71), 0),
        "attn_gain": jnp.clip(1.0 + 0.18 * jax.random.normal(seeds[2], (EMBED_WIDTH,), jnp.float32), 0.099609375, 1.8984375).astype(jnp.bfloat16),
        "query_w": scatter_about(seeds[3], (EMBED_WIDTH, QUERY_HEADS * HEAD_SIZE), EMBED_WIDTH ** -0.5, 0.1875, ((0, 8), (1, 4))),
        "key_w": scatter_about(seeds[4], (EMBED_WIDTH, KEY_VALUE_HEADS * HEAD_SIZE), EMBED_WIDTH ** -0.5, 0.1875, ((0, 8), (1, 4))),
        "value_weight": scatter_about(seeds[5], (EMBED_WIDTH, KEY_VALUE_HEADS * HEAD_SIZE), EMBED_WIDTH ** -0.5, 0.1875, ((0, 8), (1, 4))),
        "output_weight": scatter_about(seeds[6], (QUERY_HEADS * HEAD_SIZE, EMBED_WIDTH), (max(1, QUERY_HEADS * HEAD_SIZE // 256)) ** -0.5, 3.5, ((0, 8), (1, 4))),
        "ffn_gain": jnp.clip(1.0 + 0.18 * jax.random.normal(seeds[7], (EMBED_WIDTH,), jnp.float32), 0.099609375, 1.8984375).astype(jnp.bfloat16),
        "gate_w": scatter_about(seeds[8], (EMBED_WIDTH, FF), EMBED_WIDTH ** -0.5, 0.1875, ((0, 8), (1, 4))),
        "up_w": scatter_about(seeds[9], (EMBED_WIDTH, FF), EMBED_WIDTH ** -0.5, 0.1875, ((0, 8), (1, 4))),
        "down_w": scatter_about(seeds[10], (FF, EMBED_WIDTH), FF ** -0.5, 0.125, ((0, 8), (1, 4))),
        "cotangent": scatter_about(seeds[11], (SEQS, SEQ_LEN, EMBED_WIDTH), 1.0, 6.0, ((0, 4), (1, 8))),
    }


eps = 1e-05
rope_base = 10000.0

def to_bfloat(tensor):
    return lax.optimization_barrier(tensor.astype(jnp.bfloat16)).astype(jnp.float32)

def rope_tables(places, head_width):
    half_width = head_width // 2
    frequency = jnp.power(rope_base, -2.0 * jnp.arange(half_width, dtype=jnp.float32) / head_width)
    angles = places.astype(jnp.float32)[:, None] * frequency[None, :]
    return (jnp.cos(angles)[:, None, :], jnp.sin(angles)[:, None, :])

def apply_rotation(tensor, cosine_table, sinusoid_table):
    half_width = tensor.shape[-1] // 2
    first_half = tensor[..., :half_width]
    second_half = tensor[..., half_width:]
    return jnp.concatenate([first_half * cosine_table - second_half * sinusoid_table, second_half * cosine_table + first_half * sinusoid_table], axis=-1)

def inverse_rotation(tensor, cosine_table, sinusoid_table):
    half_width = tensor.shape[-1] // 2
    first_half = tensor[..., :half_width]
    second_half = tensor[..., half_width:]
    return jnp.concatenate([first_half * cosine_table + second_half * sinusoid_table, second_half * cosine_table - first_half * sinusoid_table], axis=-1)

def outer_sum(left_rows, right_rows):
    return lax.dot_general(left_rows, right_rows, (((0,), (0,)), ((), ())), preferred_element_type=jnp.float32)

def reverse_projection(grad_rows, weight):
    return lax.dot_general(grad_rows, weight, (((1,), (1,)), ((), ())), preferred_element_type=jnp.float32)

def attend_forward(queries, key_rows, values, places):
    sequence_length = queries.shape[0]
    block_rows = min(512, sequence_length)
    block_count = sequence_length // block_rows
    key_float = key_rows.astype(jnp.float32)
    value_float = values.astype(jnp.float32)
    factor = queries.shape[-1] ** (-0.5)

    def one_block(number):
        offset = number * block_rows
        query_block = lax.dynamic_slice_in_dim(queries, offset, block_rows, 0).astype(jnp.float32)
        query_places = lax.dynamic_slice_in_dim(places, offset, block_rows, 0)
        scores = jnp.einsum('qhgd,khd->hgqk', query_block, key_float) * factor
        allowed = places[None, None, None, :] <= query_places[None, None, :, None]
        scores = jnp.where(allowed, scores, -jnp.inf)
        log_total = jax.nn.logsumexp(scores, axis=-1)
        weights = to_bfloat(jnp.where(allowed, jnp.exp(scores - log_total[..., None]), 0.0))
        mixture = jnp.einsum('hgqk,khd->qhgd', weights, value_float)
        return (mixture, log_total)
    mixture, log_total = lax.map(one_block, jnp.arange(block_count, dtype=jnp.int32))
    return (mixture.reshape(queries.shape), log_total)

def attend_backward(queries, key_rows, values, places, out_bf, grad_bf, log_total):
    sequence_length = queries.shape[0]
    block_rows = min(512, sequence_length)
    block_count = sequence_length // block_rows
    key_float = key_rows.astype(jnp.float32)
    value_float = values.astype(jnp.float32)
    factor = queries.shape[-1] ** (-0.5)

    def one_block(carry, number):
        key_gradient, value_gradient = carry
        offset = number * block_rows
        query_block = lax.dynamic_slice_in_dim(queries, offset, block_rows, 0).astype(jnp.float32)
        query_places = lax.dynamic_slice_in_dim(places, offset, block_rows, 0)
        out_block = lax.dynamic_slice_in_dim(out_bf, offset, block_rows, 0).astype(jnp.float32)
        grad_block = lax.dynamic_slice_in_dim(grad_bf, offset, block_rows, 0).astype(jnp.float32)
        scores = jnp.einsum('qhgd,khd->hgqk', query_block, key_float) * factor
        allowed = places[None, None, None, :] <= query_places[None, None, :, None]
        scores = jnp.where(allowed, scores, -jnp.inf)
        weights = jnp.where(allowed, jnp.exp(scores - log_total[number][..., None]), 0.0)
        weight_bf = to_bfloat(weights)
        value_gradient = value_gradient + jnp.einsum('hgqk,qhgd->khd', weight_bf, grad_block)
        weight_grad = jnp.einsum('qhgd,khd->hgqk', grad_block, value_float)
        delta_rows = jnp.einsum('qhgd,qhgd->hgq', grad_block, out_block)
        score_grad = to_bfloat(weights * (weight_grad - delta_rows[..., None]))
        query_grad = jnp.einsum('hgqk,khd->qhgd', score_grad, key_float) * factor
        key_gradient = key_gradient + jnp.einsum('hgqk,qhgd->khd', score_grad, query_block) * factor
        return ((key_gradient, value_gradient), query_grad)
    start_carry = (jnp.zeros(key_rows.shape, jnp.float32), jnp.zeros(values.shape, jnp.float32))
    (key_gradient, value_gradient), query_grad = lax.scan(one_block, start_carry, jnp.arange(block_count, dtype=jnp.int32))
    return (query_grad.reshape(queries.shape), key_gradient, value_gradient)

def reference(hidden_in, positions, attn_gain, query_w, key_w, value_weight, output_weight, ffn_gain, gate_w, up_w, down_w, cotangent):
    query_group_width = QUERY_HEADS // KEY_VALUE_HEADS
    gain_one = attn_gain.astype(jnp.float32)
    gain_two = ffn_gain.astype(jnp.float32)
    grad_scale = float(hidden_in.shape[0] * hidden_in.shape[1]) ** (-0.5)

    def one_sequence(carry, inputs):
        tokens, places, cot_rows = inputs
        sequence_length = tokens.shape[0]
        x_float = tokens.astype(jnp.float32)
        inv_one = lax.rsqrt(lax.optimization_barrier(jnp.mean(x_float * x_float, axis=-1, keepdims=True)) + eps)
        normed_one = (x_float * inv_one * gain_one).astype(jnp.bfloat16)
        query_pre = jnp.dot(normed_one, query_w, preferred_element_type=jnp.float32)
        key_before_rotation = jnp.dot(normed_one, key_w, preferred_element_type=jnp.float32)
        value_before_cast = jnp.dot(normed_one, value_weight, preferred_element_type=jnp.float32)
        cosine_table, sinusoid_table = rope_tables(places, HEAD_SIZE)
        query_bfloat = apply_rotation(query_pre.reshape(sequence_length, QUERY_HEADS, HEAD_SIZE), cosine_table, sinusoid_table).astype(jnp.bfloat16)
        query_bfloat = query_bfloat.reshape(sequence_length, KEY_VALUE_HEADS, query_group_width, HEAD_SIZE)
        key_bfloat = apply_rotation(key_before_rotation.reshape(sequence_length, KEY_VALUE_HEADS, HEAD_SIZE), cosine_table, sinusoid_table).astype(jnp.bfloat16)
        value_bfloat = value_before_cast.reshape(sequence_length, KEY_VALUE_HEADS, HEAD_SIZE).astype(jnp.bfloat16)
        mixture, log_total = attend_forward(query_bfloat, key_bfloat, value_bfloat, places)
        mix_bf = mixture.astype(jnp.bfloat16)
        mix_flat = mix_bf.reshape(sequence_length, QUERY_HEADS * HEAD_SIZE)
        middle = x_float + jnp.dot(mix_flat, output_weight, preferred_element_type=jnp.float32)
        inv_two = lax.rsqrt(lax.optimization_barrier(jnp.mean(middle * middle, axis=-1, keepdims=True)) + eps)
        normed_two = (middle * inv_two * gain_two).astype(jnp.bfloat16)
        gate_pre = jnp.dot(normed_two, gate_w, preferred_element_type=jnp.float32)
        up_pre = jnp.dot(normed_two, up_w, preferred_element_type=jnp.float32)
        sigma = jax.nn.sigmoid(gate_pre)
        act_bf = (gate_pre * sigma * up_pre).astype(jnp.bfloat16)
        output = middle + jnp.dot(act_bf, down_w, preferred_element_type=jnp.float32)
        cot_float = cot_rows.astype(jnp.float32)
        grad_down = outer_sum(act_bf, cot_rows)
        act_grad = reverse_projection(cot_rows, down_w)
        gate_grad = (act_grad * up_pre * sigma * (1.0 + gate_pre * (1.0 - sigma))).astype(jnp.bfloat16)
        up_grad = (act_grad * gate_pre * sigma).astype(jnp.bfloat16)
        grad_gate = outer_sum(normed_two, gate_grad)
        grad_up = outer_sum(normed_two, up_grad)
        norm_two_grad = reverse_projection(gate_grad, gate_w) + reverse_projection(up_grad, up_w)
        grad_gain_two = lax.optimization_barrier(jnp.sum(norm_two_grad * middle * inv_two, axis=0))
        scaled_two = gain_two * norm_two_grad
        middle_grad = cot_float + inv_two * (scaled_two - middle * inv_two * inv_two * lax.optimization_barrier(jnp.mean(scaled_two * middle, axis=-1, keepdims=True)))
        middle_bfloat = middle_grad.astype(jnp.bfloat16)
        grad_out = outer_sum(mix_flat, middle_bfloat)
        mixing_gradient = reverse_projection(middle_bfloat, output_weight).astype(jnp.bfloat16).reshape(sequence_length, KEY_VALUE_HEADS, query_group_width, HEAD_SIZE)
        query_grad, key_gradient, value_gradient = attend_backward(query_bfloat, key_bfloat, value_bfloat, places, mix_bf, mixing_gradient, log_total)
        query_gbf = inverse_rotation(query_grad.reshape(sequence_length, QUERY_HEADS, HEAD_SIZE), cosine_table, sinusoid_table).astype(jnp.bfloat16).reshape(sequence_length, QUERY_HEADS * HEAD_SIZE)
        key_gradient_bfloat = inverse_rotation(key_gradient, cosine_table, sinusoid_table).astype(jnp.bfloat16).reshape(sequence_length, KEY_VALUE_HEADS * HEAD_SIZE)
        value_gradient_bfloat = value_gradient.astype(jnp.bfloat16).reshape(sequence_length, KEY_VALUE_HEADS * HEAD_SIZE)
        grad_query = outer_sum(normed_one, query_gbf)
        grad_key = outer_sum(normed_one, key_gradient_bfloat)
        grad_value = outer_sum(normed_one, value_gradient_bfloat)
        norm_one_grad = reverse_projection(query_gbf, query_w) + reverse_projection(key_gradient_bfloat, key_w) + reverse_projection(value_gradient_bfloat, value_weight)
        grad_gain_one = lax.optimization_barrier(jnp.sum(norm_one_grad * x_float * inv_one, axis=0))
        scaled_one = gain_one * norm_one_grad
        input_grad = middle_grad + inv_one * (scaled_one - x_float * inv_one * inv_one * lax.optimization_barrier(jnp.mean(scaled_one * x_float, axis=-1, keepdims=True)))
        terms = (grad_gain_one, grad_query, grad_key, grad_value, grad_out, grad_gain_two, grad_gate, grad_up, grad_down)
        carry = tuple((total + term for total, term in zip(carry, terms)))
        return (carry, (output, input_grad))
    start_carry = (jnp.zeros(attn_gain.shape, jnp.float32), jnp.zeros(query_w.shape, jnp.float32), jnp.zeros(key_w.shape, jnp.float32), jnp.zeros(value_weight.shape, jnp.float32), jnp.zeros(output_weight.shape, jnp.float32), jnp.zeros(ffn_gain.shape, jnp.float32), jnp.zeros(gate_w.shape, jnp.float32), jnp.zeros(up_w.shape, jnp.float32), jnp.zeros(down_w.shape, jnp.float32))
    sums, (hidden_out, grad_in) = lax.scan(one_sequence, start_carry, (hidden_in, positions, cotangent))
    sums = tuple((total * grad_scale for total in sums))
    return (hidden_out, grad_in, sums[0], sums[1], sums[2], sums[3], sums[4], sums[5], sums[6], sums[7], sums[8])
```

```python
import functools

import jax
import jax.numpy as jnp
from jax import lax
from jax.experimental import pallas as pl
from jax.experimental.pallas import tpu as pltpu
from jax.sharding import PartitionSpec as P

QH = 15
KVH = 5
HD = 64
GRP = QH // KVH
KVW = KVH * HD
SPLIT = 256
eps = 1e-05
rope_base = 10000.0
neg_big = -1e30
AX = ("dp", "ctx")
f32 = jnp.float32
bf16 = jnp.bfloat16


def moved(x, nd, nc, target):
    table = []
    for d in range(nd):
        for c in range(nc):
            dd, cc = target(d, c)
            table.append((d * nc + c, dd * nc + cc))
    return lax.ppermute(x, AX, table)


def swapped(x, nd, nc, dx, cy):
    return moved(x, nd, nc, lambda d, c: (d ^ dx, c ^ cy))


def from_line(x, nd, nc, k):
    length = nc // 2
    return moved(x, nd, nc, lambda d, c: (d, 2 * ((c // 2 - k) % length) + c % 2))


def line_gather(x, nd, nc, l):
    length = nc // 2
    out = jnp.zeros((length,) + x.shape, x.dtype)
    for k in range(length):
        piece = x if k == 0 else from_line(x, nd, nc, k)
        out = lax.dynamic_update_index_in_dim(out, piece, lax.rem(l + k, length), 0)
    return out


def line_scatter(x, nd, nc, l):
    length = nc // 2
    total = lax.dynamic_index_in_dim(x, l, 0, keepdims=False).astype(f32)
    for k in range(1, length):
        piece = lax.dynamic_index_in_dim(x, lax.rem(l + k, length), 0, keepdims=False)
        total = total + from_line(piece.astype(bf16), nd, nc, -k).astype(f32)
    return total


SLOTS = ((0, 0), (2, 0), (0, 1), (2, 1))


def slab_gather(x, nd, nc):
    mine = [x] + [swapped(x, nd, nc, dx, cy) for dx, cy in SLOTS[1:]]
    other = [swapped(p, nd, nc, 1, 0) for p in mine]
    return mine + other


def slab_scatter(mine, other, nd, nc):
    got = swapped(other.astype(bf16), nd, nc, 1, 0)
    part = mine + got.astype(f32)
    total = part[0]
    for i in (3, 1, 2):
        dx, cy = SLOTS[i]
        total = total + swapped(part[i].astype(bf16), nd, nc, dx, cy).astype(f32)
    return total


def head_rows(ref, h, tokens):
    return jnp.concatenate(
        [ref[:, HD * (GRP * h + g) : HD * (GRP * h + g + 1)] for g in range(GRP)], axis=0
    )


def key_places(starts_ref, i, tokens):
    row = lax.broadcasted_iota(jnp.int32, (tokens, 1), 0)
    half = tokens // 2
    return jnp.where(row < half, starts_ref[i, 0] + row, starts_ref[i, 1] + row - half)


def nt(a, b):
    return lax.dot_general(a, b, (((1,), (1,)), ((), ())), preferred_element_type=f32)


def nn(a, b):
    return lax.dot_general(a, b, (((1,), (0,)), ((), ())), preferred_element_type=f32)


def tn(a, b):
    return lax.dot_general(a, b, (((0,), (0,)), ((), ())), preferred_element_type=f32)


def forward_kernel(starts_ref, places_ref, q_ref, kv_ref, mix_ref, lse_ref, s_ref):
    chunks, tokens, _ = kv_ref.shape
    places = places_ref[...]
    for h in range(KVH):
        qh = head_rows(q_ref, h, tokens)
        top = jnp.full((1, GRP * tokens), neg_big, f32)
        for i in range(chunks):
            s = nt(kv_ref[i, :, HD * h : HD * (h + 1)], qh) * (HD**-0.5)
            s = jnp.where(key_places(starts_ref, i, tokens) <= places, s, neg_big)
            s_ref[i] = s
            top = jnp.maximum(top, jnp.max(s, axis=0, keepdims=True))
        total = jnp.zeros((1, GRP * tokens), f32)
        for i in range(chunks):
            e = jnp.exp(s_ref[i] - top)
            s_ref[i] = e
            total = total + jnp.sum(e, axis=0, keepdims=True)
        lse_ref[h : h + 1, :] = top + jnp.log(total)
        scale = 1.0 / total
        out = jnp.zeros((HD, GRP * tokens), f32)
        for i in range(chunks):
            p = (s_ref[i] * scale).astype(bf16)
            out = out + tn(kv_ref[i, :, KVW + HD * h : KVW + HD * (h + 1)], p)
        rows = out.T.astype(bf16)
        for g in range(GRP):
            n = GRP * h + g
            mix_ref[:, HD * n : HD * (n + 1)] = rows[tokens * g : tokens * (g + 1)]


def backward_kernel(
    starts_ref, places_ref, q_ref, kv_ref, lse_ref, mix_ref, grad_ref, dq_ref, dkv_ref
):
    chunks, tokens, _ = kv_ref.shape
    places = places_ref[...]
    factor = HD**-0.5
    for h in range(KVH):
        qh = head_rows(q_ref, h, tokens)
        gh = head_rows(grad_ref, h, tokens)
        oh = head_rows(mix_ref, h, tokens)
        delta = jnp.sum((gh.astype(f32) * oh.astype(f32)).T, axis=0, keepdims=True)
        lse = lse_ref[h : h + 1, :]
        dq = jnp.zeros((GRP * tokens, HD), f32)
        for i in range(chunks):
            k = kv_ref[i, :, HD * h : HD * (h + 1)]
            v = kv_ref[i, :, KVW + HD * h : KVW + HD * (h + 1)]
            s = nt(k, qh) * factor
            p = jnp.where(key_places(starts_ref, i, tokens) <= places, jnp.exp(s - lse), 0.0)
            dv = nn(p.astype(bf16), gh)
            ds = (p * (nt(v, gh) - delta)).astype(bf16)
            dk = nn(ds, qh) * factor
            dq = dq + tn(ds, k)
            dkv_ref[i, :, HD * h : HD * (h + 1)] = dk.astype(dkv_ref.dtype)
            dkv_ref[i, :, KVW + HD * h : KVW + HD * (h + 1)] = dv.astype(dkv_ref.dtype)
        dq = dq * factor
        for g in range(GRP):
            n = GRP * h + g
            dq_ref[:, HD * n : HD * (n + 1)] = dq[tokens * g : tokens * (g + 1)]


VM = pl.BlockSpec(memory_space=pltpu.VMEM)
SM = pl.BlockSpec(memory_space=pltpu.SMEM)


def attend_forward(starts, places, q, kv):
    chunks, tokens, _ = kv.shape
    wide = GRP * tokens
    return pl.pallas_call(
        forward_kernel,
        out_shape=(
            jax.ShapeDtypeStruct(q.shape, bf16),
            jax.ShapeDtypeStruct((8, wide), f32),
        ),
        in_specs=[SM, VM, VM, VM],
        out_specs=(VM, VM),
        scratch_shapes=[pltpu.VMEM((chunks, tokens, wide), f32)],
        compiler_params=pltpu.CompilerParams(vmem_limit_bytes=48 << 20),
        cost_estimate=pl.CostEstimate(
            flops=4 * chunks * tokens * tokens * QH * HD,
            transcendentals=chunks * tokens * tokens * QH,
            bytes_accessed=2 * (q.size + kv.size),
        ),
        name="attend_forward",
    )(starts, places, q, kv)


def attend_backward(starts, places, q, kv, lse, mix, grad):
    chunks, tokens, width = kv.shape
    return pl.pallas_call(
        backward_kernel,
        out_shape=(
            jax.ShapeDtypeStruct(q.shape, f32),
            jax.ShapeDtypeStruct(kv.shape, bf16),
        ),
        in_specs=[SM, VM, VM, VM, VM, VM, VM],
        out_specs=(VM, VM),
        compiler_params=pltpu.CompilerParams(vmem_limit_bytes=48 << 20),
        cost_estimate=pl.CostEstimate(
            flops=10 * chunks * tokens * tokens * QH * HD,
            transcendentals=chunks * tokens * tokens * QH,
            bytes_accessed=2 * (2 * q.size + 2 * kv.size),
        ),
        name="attend_backward",
    )(starts, places, q, kv, lse, mix, grad)


def rope_rows(places, heads):
    half = HD // 2
    frequency = jnp.power(rope_base, -2.0 * jnp.arange(half, dtype=f32) / HD)
    angles = places.astype(f32)[:, None] * frequency[None, :]
    c, s = jnp.cos(angles), jnp.sin(angles)
    return (
        jnp.tile(jnp.concatenate([c, c], axis=1), (1, heads)),
        jnp.tile(jnp.concatenate([-s, s], axis=1), (1, heads)),
    )


def halves_swapped(x):
    lane = lax.broadcasted_iota(jnp.int32, x.shape, 1)
    return jnp.where(lane % HD < HD // 2, jnp.roll(x, -(HD // 2), 1), jnp.roll(x, HD // 2, 1))


def rotated(x, c, s):
    return x * c[:, : x.shape[1]] + halves_swapped(x) * s[:, : x.shape[1]]


def by_bit(bit, zero, one):
    return jnp.where(bit == 0, zero, one)


def columns(x):
    return jnp.concatenate([x[i] for i in range(x.shape[0])], axis=1)


def on_device(
    nd, nc, hidden_in, positions, attn_gain, query_w, key_w, value_w, output_w,
    ffn_gain, gate_w, up_w, down_w, cotangent,
):
    _, tokens, width = hidden_in.shape
    length = nc // 2
    d0, c0 = lax.axis_index("dp"), lax.axis_index("ctx")
    l0, y0 = c0 // 2, lax.rem(c0, 2)
    rows = width // nc
    qw, kw = query_w.shape[1], key_w.shape[1]
    ffd = gate_w.shape[1]
    units = ffd // 2
    down_rows = down_w.shape[0]
    fold = nc // (2 * nd)
    grad_scale = float(tokens * nd * nc) ** (-0.5)
    gather = functools.partial(line_gather, nd=nd, nc=nc, l=l0)
    scatter = functools.partial(line_scatter, nd=nd, nc=nc, l=l0)

    part_q = SPLIT - 2 * kw
    first = jnp.concatenate([key_w, value_w, query_w[:, :part_q]], axis=1)
    second = jnp.concatenate([query_w[:, part_q:], output_w], axis=1)

    def everywhere(shard):
        pieces = slab_gather(gather(shard), nd, nc)
        out = jnp.zeros((nd, length, 2) + shard.shape, shard.dtype)
        for n, piece in enumerate(pieces):
            dx, cy = SLOTS[n % 4]
            at = (d0 ^ (dx + n // 4), 0, y0 ^ cy, 0, 0)
            out = lax.dynamic_update_slice(out, piece[None, :, None], at)
        return out.reshape(nd, width, shard.shape[1])

    first_full = everywhere(first)

    half = tokens // 2
    numbers = jnp.stack([positions[0, 0], positions[0, half]]).astype(f32) / half
    small = jnp.concatenate([attn_gain, ffn_gain, numbers.astype(bf16)])
    small = lax.all_gather(small, "ctx", axis=0)
    gain_one = small[:, :rows].reshape(1, width).astype(f32)
    gain_two = small[:, rows : 2 * rows].reshape(1, width).astype(f32)
    starts = (small[:, 2 * rows :].astype(f32) * half).astype(jnp.int32)
    order = [2 * lax.rem(l0 + k, length) + (y0 ^ cy) for cy in (0, 1) for k in range(length)]
    starts = jnp.take(starts, jnp.stack(order), axis=0)
    places = positions[0]
    wide_places = jnp.tile(places[None, :], (1, GRP))
    c_rows, s_rows = rope_rows(places, QH)

    x = hidden_in[0].astype(f32)
    inv_one = lax.rsqrt(jnp.mean(x * x, axis=-1, keepdims=True) + eps)
    normed_one = (x * inv_one * gain_one).astype(bf16)

    def own_half(w, y):
        return by_bit(y, w[:, :units], w[:, units:])

    keep = jnp.concatenate([own_half(gate_w, y0), own_half(up_w, y0)], axis=1)
    give = jnp.concatenate([own_half(gate_w, 1 - y0), own_half(up_w, 1 - y0)], axis=1)
    take = swapped(give, nd, nc, 0, 1)
    gate_up = jnp.concatenate([by_bit(y0, keep, take), by_bit(y0, take, keep)], axis=0)

    def down_target(d, c):
        t, i = c // fold, c % fold
        return t // 2, 2 * (fold * d + i) + t % 2

    down_back = {down_target(d, c): (d, c) for d in range(nd) for c in range(nc)}
    down_t = moved(down_w.T, nd, nc, down_target)
    if fold == 1:
        ffn = gather(jnp.concatenate([gate_up, down_t], axis=1)).reshape(width, 3 * units)
        gu_w, dt_w = ffn[:, : 2 * units], ffn[:, 2 * units :]
    else:
        gu_w = gather(gate_up).reshape(width, 2 * units)
        dt_w = gather(down_t).reshape(nd, fold, width // nd, down_rows)
        dt_w = dt_w.transpose(0, 2, 1, 3).reshape(width, units)

    one = jnp.einsum("tf,dfn->dtn", normed_one, first_full, preferred_element_type=f32)
    k = rotated(columns(one[:, :, :kw]), c_rows, s_rows)
    v = columns(one[:, :, kw : 2 * kw])
    kv_own = jnp.concatenate([k, v], axis=1).astype(bf16)
    along = [kv_own] + [from_line(kv_own, nd, nc, k) for k in range(1, length)]
    kv = jnp.stack(along + [swapped(p, nd, nc, 0, 1) for p in along])

    second_full = everywhere(second)
    rest_q = qw - part_q
    two = jnp.einsum("tf,dfn->dtn", normed_one, second_full[:, :, :rest_q], preferred_element_type=f32)
    q = rotated(columns(jnp.concatenate([one[:, :, 2 * kw :], two], axis=2)), c_rows, s_rows)
    q = q.astype(bf16)
    wo = second_full[:, :, rest_q:]

    mix, lse = attend_forward(starts, wide_places, q, kv)

    mid = x + columns(jnp.einsum("tf,dfn->dtn", mix, wo, preferred_element_type=f32))
    inv_two = lax.rsqrt(jnp.mean(mid * mid, axis=-1, keepdims=True) + eps)
    normed_two = (mid * inv_two * gain_two).astype(bf16)

    cot = jnp.concatenate(slab_gather(cotangent[0], nd, nc), axis=0)
    n2 = jnp.concatenate(slab_gather(normed_two, nd, nc), axis=0)
    act_grad = nn(cot, dt_w)
    gate_up_out = nn(n2, gu_w)
    gate, up = gate_up_out[:, :units], gate_up_out[:, units:]
    sigma = jax.nn.sigmoid(gate)
    act = (gate * sigma * up).astype(bf16)
    gate_grad = act_grad * up * sigma * (1.0 + gate * (1.0 - sigma))
    up_grad = act_grad * gate * sigma
    gu_grad = jnp.concatenate([gate_grad, up_grad], axis=1).astype(bf16)

    def home(partial):
        partial = partial.reshape(2, 4, tokens, width)
        return slab_scatter(partial[0], partial[1], nd, nc)

    norm_two_grad = home(nt(gu_grad, gu_w))
    hidden_out = mid + home(nt(act, dt_w))

    d_gu, d_dt = tn(n2, gu_grad), tn(cot, act)
    if fold == 1:
        summed = scatter(jnp.concatenate([d_gu, d_dt], axis=1).reshape(length, 2 * rows, 3 * units))
        s_gu, s_dt = summed[:, : 2 * units], summed[:, 2 * units :]
    else:
        s_gu = scatter(d_gu.reshape(length, 2 * rows, 2 * units))
        d_dt = d_dt.reshape(nd, width // nd, fold, down_rows).transpose(0, 2, 1, 3)
        s_dt = scatter(d_dt.reshape(length, width // nd, down_rows))
    s_gu = s_gu * grad_scale
    mine = by_bit(y0, s_gu[:rows], s_gu[rows:])
    theirs = swapped(by_bit(y0, s_gu[rows:], s_gu[:rows]).astype(bf16), nd, nc, 0, 1).astype(f32)
    low, high = by_bit(y0, mine, theirs), by_bit(y0, theirs, mine)
    grad_gate = jnp.concatenate([low[:, :units], high[:, :units]], axis=1)
    grad_up = jnp.concatenate([low[:, units:], high[:, units:]], axis=1)
    s_dt = moved((s_dt * grad_scale).astype(bf16), nd, nc, lambda d, c: down_back[(d, c)])
    grad_down = s_dt.T.astype(f32)

    gain_two_terms = jnp.sum(norm_two_grad * mid * inv_two, axis=0)
    u2 = gain_two * norm_two_grad
    mid_grad = cotangent[0].astype(f32) + inv_two * (
        u2 - mid * inv_two * inv_two * jnp.mean(u2 * mid, axis=-1, keepdims=True)
    )
    mid_bf = mid_grad.astype(bf16)
    mid_blocks = jnp.stack([mid_bf[:, qw * i : qw * (i + 1)] for i in range(nd)])
    mix_grad = jnp.einsum("dtn,dfn->tf", mid_blocks, wo, preferred_element_type=f32).astype(bf16)

    dq, dkv = attend_backward(starts, wide_places, q, kv, lse, mix, mix_grad)

    came = swapped(dkv[length:], nd, nc, 0, 1)
    part = dkv[:length].astype(f32) + came.astype(f32)
    dkv_sum = part[0]
    for k in range(1, length):
        dkv_sum = dkv_sum + from_line(part[k].astype(bf16), nd, nc, -k).astype(f32)

    dq = rotated(dq, c_rows, -s_rows).astype(bf16)
    dk = rotated(dkv_sum[:, :KVW], c_rows, -s_rows).astype(bf16)
    dv = dkv_sum[:, KVW:].astype(bf16)

    def blocks(a, w):
        return jnp.stack([a[:, w * i : w * (i + 1)] for i in range(nd)])

    dq_b = blocks(dq, qw)
    one_grad = jnp.concatenate([blocks(dk, kw), blocks(dv, kw), dq_b[:, :, :part_q]], axis=2)
    two_grad = jnp.concatenate([dq_b[:, :, part_q:], mid_blocks], axis=2)
    norm_one_grad = jnp.einsum(
        "dtn,dfn->tf", two_grad[:, :, :rest_q], second_full[:, :, :rest_q], preferred_element_type=f32
    ) + jnp.einsum("dtn,dfn->tf", one_grad, first_full, preferred_element_type=f32)
    gain_one_terms = jnp.sum(norm_one_grad * x * inv_one, axis=0)
    u1 = gain_one * norm_one_grad
    grad_in = mid_grad + inv_one * (
        u1 - x * inv_one * inv_one * jnp.mean(u1 * x, axis=-1, keepdims=True)
    )

    def to_owner(term):
        def cut(a):
            return a.reshape(length, 2, a.shape[0] // nc, a.shape[1])

        other = [cut(term(d0 ^ dx ^ 1)).astype(bf16) for dx in (0, 2)]
        own = [cut(term(d0 ^ dx)) for dx in (0, 2)]
        got = swapped(jnp.stack(other), nd, nc, 1, 0)
        part = [a + got[n].astype(f32) for n, a in enumerate(own)]

        def at(n, y):
            return lax.dynamic_index_in_dim(part[n], y, 1, keepdims=False)

        total = at(0, y0)
        for dx, cy in SLOTS[1:]:
            piece = at(dx // 2, y0 ^ cy).astype(bf16)
            total = total + swapped(piece, nd, nc, dx, cy).astype(f32)
        return scatter(total)

    def pick(a, d):
        return lax.dynamic_index_in_dim(a, d, 0, keepdims=False)

    def second_term(d):
        block = pick(two_grad, d)
        return jnp.concatenate(
            [tn(normed_one, block[:, :rest_q]), tn(mix, block[:, rest_q:])], axis=1
        )

    extra = 8 if rows % 8 == 0 else -rows % 8
    gains = jnp.concatenate(
        [gain_one_terms.reshape(nc, 1, rows), gain_two_terms.reshape(nc, 1, rows)], axis=2
    )
    gains = jnp.pad(gains, ((0, 0), (0, extra - 1), (0, SPLIT - 2 * rows)))

    def first_term(d):
        w = tn(normed_one, pick(one_grad, d)).reshape(nc, rows, SPLIT)
        return jnp.concatenate([w, gains], axis=1).reshape(nc * (rows + extra), SPLIT)

    sum_two = to_owner(second_term) * grad_scale
    sum_one = to_owner(first_term) * grad_scale
    grad_query = jnp.concatenate([sum_one[:rows, 2 * kw :], sum_two[:, :rest_q]], axis=1)
    return (
        hidden_out[None],
        grad_in[None],
        sum_one[rows, :rows],
        grad_query,
        sum_one[:rows, :kw],
        sum_one[:rows, kw : 2 * kw],
        sum_two[:, rest_q:],
        sum_one[rows, rows : 2 * rows],
        grad_gate,
        grad_up,
        grad_down,
    )


def solution(mesh):
    nd, nc = mesh.shape["dp"], mesh.shape["ctx"]
    whole, rows, gain = P("dp", "ctx", None), P("ctx", "dp"), P("ctx")
    in_specs = (whole, P("dp", "ctx"), gain, rows, rows, rows, rows, gain, rows, rows, rows, whole)
    out_specs = (whole, whole, gain, rows, rows, rows, rows, gain, rows, rows, rows)
    return jax.shard_map(
        functools.partial(on_device, nd, nc),
        mesh=mesh,
        in_specs=in_specs,
        out_specs=out_specs,
        check_vma=False,
    )
```

```python
import functools
from types import SimpleNamespace

import jax
import jax.numpy as jnp
from jax import lax
from jax.experimental import pallas as pl
from jax.experimental.pallas import tpu as pltpu
from jax.sharding import PartitionSpec as P


QH = 15
KVH = 5
HD = 64
HALF = HD // 2
GRP = QH // KVH
KVW = KVH * HD
eps = 1e-05
rope_base = 10000.0
neg_big = -1e30
AX = ("dp", "ctx")
f32 = jnp.float32
bf16 = jnp.bfloat16


SLOTS = ((0, 0), (1, 0), (0, 1), (1, 1))


def moved(z, x, target):
    table = []
    for d in range(z.nd):
        for c in range(z.nc):
            dd, cc = target(d, c)
            table.append((d * z.nc + c, dd * z.nc + cc))
    return lax.ppermute(x, AX, table)


def to_slot(z, x, i):
    fx, fy = SLOTS[i]
    return moved(z, x, lambda d, c: (d ^ (2 * fx), c ^ fy))


def to_core(z, x):
    return moved(z, x, lambda d, c: (d ^ 1, c))


def from_line(z, x, k):
    return moved(z, x, lambda d, c: (d, 2 * ((c // 2 - k) % z.length) + c % 2))


def inner(z, x, toward_middle, outward):
    table = []
    for d in range(z.nd):
        for c in range(z.nc):
            l = c // 2
            to = {1: 2, 2: 1} if not outward else {1: 0, 2: 3}
            if outward and toward_middle:
                to = {0: 1, 3: 2}
            if l in to:
                table.append((d * z.nc + c, d * z.nc + 2 * to[l] + c % 2))
    return lax.ppermute(x, AX, table)


def line_pieces(z, x):
    L = z.length
    if L != 4:
        return [x] + [from_line(z, x, k) for k in range(1, L)]
    one, three = from_line(z, x, 1), from_line(z, x, 3)
    l = lax.axis_index("ctx") // 2
    out = jnp.where(l == 1, one, three)
    across = jnp.where(l == 1, three, one)
    p = inner(z, out, False, True)
    q = inner(z, across, False, False)
    return [x, one, jnp.where((l == 0) | (l == 3), p, q), three]


def nt(a, b):
    return lax.dot_general(a, b, (((1,), (1,)), ((), ())), preferred_element_type=f32)


def nn(a, b):
    return lax.dot_general(a, b, (((1,), (0,)), ((), ())), preferred_element_type=f32)


def tn(a, b):
    return lax.dot_general(a, b, (((0,), (0,)), ((), ())), preferred_element_type=f32)


def place():
    d0, c0 = lax.axis_index("dp"), lax.axis_index("ctx")
    return SimpleNamespace(x=d0 // 2, core=lax.rem(d0, 2), l=c0 // 2, y=lax.rem(c0, 2))


def flip(bit, f):
    return 1 - bit if f else bit


def d_of(at, fx, fcore):
    return 2 * flip(at.x, fx) + flip(at.core, fcore)


def c_of(z, at, fy, k):
    return 2 * lax.rem(at.l + k, z.length) + flip(at.y, fy)


def pieces_of(pieces, fy):
    return [(pieces[4 * fcore + fx + 2 * fy], fx, fcore) for fcore in (0, 1) for fx in (0, 1)]


def gathered(z, at, ref, fy):
    return jnp.concatenate([ref[c_of(z, at, fy, k)] for k in range(z.length)], axis=0)


def seen(z, at, k):
    return lax.rem(at.l + k, z.nd) if z.fold == 1 else k


VM = pl.BlockSpec(memory_space=pltpu.VMEM)


def call(kernel, z, outs, args, scratch=(), flops=0):
    moved_bytes = sum(a.size * a.dtype.itemsize for a in args)
    moved_bytes += sum(o.size * o.dtype.itemsize for o in outs)
    return pl.pallas_call(
        functools.partial(kernel, z),
        out_shape=tuple(outs),
        in_specs=[VM] * len(args),
        out_specs=tuple([VM] * len(outs)),
        scratch_shapes=list(scratch),
        compiler_params=pltpu.CompilerParams(vmem_limit_bytes=56 << 20),
        cost_estimate=pl.CostEstimate(
            flops=int(flops), transcendentals=0, bytes_accessed=int(moved_bytes)
        ),
    )(*args)


def sds(shape, dtype):
    return jax.ShapeDtypeStruct(shape, dtype)


def rotate(rows, cos, sin):
    out = []
    for i in range(rows.shape[0] // HD):
        a, b = rows[HD * i : HD * i + HALF], rows[HD * i + HALF : HD * (i + 1)]
        out += [a * cos - b * sin, b * cos + a * sin]
    return jnp.concatenate(out, axis=0)


def first_kernel(z, key_ref, value_ref, gain_one_ref, gain_two_ref, places_ref, out_ref):
    half = z.tokens // 2
    blocks = [places_ref[0:1, half * i : half * i + 1].astype(f32) * (1.0 / half) for i in (0, 1)]
    rows = [gain_one_ref[...].astype(f32), gain_two_ref[...].astype(f32)]
    rows += [jnp.broadcast_to(b, (1, z.rows)) for b in blocks]
    rows += [jnp.zeros((4, z.rows), f32)]
    out_ref[: z.kw] = key_ref[...]
    out_ref[z.kw : 2 * z.kw] = value_ref[...]
    out_ref[2 * z.kw :] = jnp.concatenate(rows, axis=0).astype(bf16)


def first_call(z, key, value, gain_one, gain_two, places):
    outs = [sds((2 * z.kw + 8, z.rows), bf16)]
    args = [key, value, gain_one[None], gain_two[None], places]
    return call(first_kernel, z, outs, args)[0]


def kv_kernel(z, x_ref, cos_ref, sin_ref, *refs):
    pieces, (kv_ref, n1_ref, inv_ref, gain_ref, small_ref, acc_ref, sum_ref) = refs[:8], refs[8:]
    at = place()
    x = x_ref[...].astype(f32)
    mean = jnp.sum(jnp.sum(x * x, axis=0), axis=0, keepdims=True) * (1.0 / z.width)
    inv = lax.rsqrt(mean + eps)
    inv_ref[...] = jnp.broadcast_to(inv, inv_ref.shape)
    w = 2 * z.kw
    for fy, n in ((0, 0), (1, 2)):
        blocks = []
        for k in range(z.length):
            c = c_of(z, at, fy, k)
            small = pieces[n][k, w : w + 8, :].astype(f32)
            small_ref[c] = small
            gain = jnp.transpose(small)
            gain_ref[c] = gain
            block = x_ref[c].astype(f32) * inv * gain[:, 0:1]
            blocks.append(block)
            weights = jnp.concatenate([p[k, :w, :] for p, _, _ in pieces_of(pieces, fy)], axis=0)
            out = nn(weights, block.astype(bf16))
            if fy == 0 and k == 0:
                sum_ref[...] = out
            else:
                sum_ref[...] += out
        n1_ref[fy] = jnp.concatenate(blocks, axis=0).astype(bf16)
    for i, (_, fx, fcore) in enumerate(pieces_of(pieces, 0)):
        acc_ref[d_of(at, fx, fcore)] = sum_ref[w * i : w * (i + 1)]
    key = jnp.concatenate([acc_ref[d, : z.kw] for d in range(z.nd)], axis=0)
    value = jnp.concatenate([acc_ref[d, z.kw :] for d in range(z.nd)], axis=0)
    kv_ref[:KVW] = rotate(key, cos_ref[...], sin_ref[...]).astype(bf16)
    kv_ref[KVW:] = value.astype(bf16)


def kv_call(z, x_c, cos, sin, pieces):
    t = z.tokens
    outs = [
        sds((2 * KVW, t), bf16),
        sds((2, z.length * z.rows, t), bf16),
        sds((8, t), f32),
        sds((z.nc, z.rows, 8), f32),
        sds((z.nc, 8, z.rows), f32),
    ]
    scratch = [pltpu.VMEM((z.nd, 2 * z.kw, t), f32), pltpu.VMEM((z.nd * 2 * z.kw, t), f32)]
    return call(kv_kernel, z, outs, [x_c, cos, sin] + pieces, scratch, 2 * t * z.width * 2 * KVW)


def q_kernel(z, n1_ref, cos_ref, sin_ref, *refs):
    pieces, (q_ref, acc_ref) = refs[:8], refs[8:]
    at = place()
    for (low, fx, fcore), (high, _, _) in zip(pieces_of(pieces, 0), pieces_of(pieces, 1)):
        out = tn(low[:, : z.qw], n1_ref[0]) + tn(high[:, : z.qw], n1_ref[1])
        acc_ref[d_of(at, fx, fcore)] = out
    q = jnp.concatenate([acc_ref[d] for d in range(z.nd)], axis=0)
    q_ref[...] = rotate(q, cos_ref[...], sin_ref[...]).astype(bf16)


def q_call(z, n1, cos, sin, pieces):
    scratch = [pltpu.VMEM((z.nd, z.qw, z.tokens), f32)]
    outs = [sds((QH * HD, z.tokens), bf16)]
    return call(q_kernel, z, outs, [n1, cos, sin] + pieces, scratch, 2 * z.tokens * z.width**2)[0]


def lay_keys(z, at, chunks, small_ref, places_ref, kv_ref, bias_ref):
    t = z.tokens
    row = lax.broadcasted_iota(jnp.int32, (t, t), 0)
    low = row < t // 2
    within = jnp.where(low, row, row - t // 2).astype(f32)
    places = places_ref[0:1, :]
    for n, chunk in enumerate(chunks):
        kv_ref[:, t * n : t * (n + 1)] = chunk[...]
        c = c_of(z, at, n // z.length, n % z.length)
        small = small_ref[c]
        start = jnp.where(low, small[2:3, 0:1], small[3:4, 0:1]) * float(t // 2)
        bias_ref[t * n : t * (n + 1), :] = jnp.where(start + within <= places, 0.0, neg_big)


def three(ref, h):
    return jnp.concatenate([head_of(ref, GRP * h + g) for g in range(GRP)], axis=1)


def scores(kv_ref, bias_ref, h, q3):
    s = tn(head_of(kv_ref, h), q3) * (HD**-0.5)
    bias = bias_ref[...]
    return s + jnp.concatenate([bias] * GRP, axis=1)


def each_head(z, body):
    if z.nc <= 8:
        for h in range(KVH):
            body(h)
    else:
        lax.fori_loop(0, KVH, lambda h, carry: (body(h), carry)[1], 0)


def head_of(ref, n):
    start = HD * n
    return ref[pl.ds(start if isinstance(n, int) else pl.multiple_of(start, HD), HD), :]


def put_head(ref, n, x):
    start = HD * n
    ref[pl.ds(start if isinstance(n, int) else pl.multiple_of(start, HD), HD), :] = x


def forward_kernel(z, small_ref, places_ref, q_ref, x_ref, gain_ref, *refs):
    n = z.nc
    chunks, pieces = refs[:n], refs[n : n + 8]
    mix_ref, rows_out_ref, lse_ref, mid_ref, inv_ref, n2_ref = refs[n + 8 : n + 14]
    kv_ref, bias_ref, rows_ref, block_ref = refs[n + 14 :]
    at = place()
    t = z.tokens
    lay_keys(z, at, chunks, small_ref, places_ref, kv_ref, bias_ref)

    def head(h):
        s = scores(kv_ref, bias_ref, h, three(q_ref, h))
        top = jnp.max(s, axis=0, keepdims=True)
        e = jnp.exp(s - top)
        total = jnp.sum(e, axis=0, keepdims=True)
        lse_ref[pl.ds(h, 1), :] = top + jnp.log(total)
        p = (e * (1.0 / total)).astype(bf16)
        out = nn(head_of(kv_ref, KVH + h), p)
        for g in range(GRP):
            put_head(rows_ref, GRP * h + g, out[:, t * g : t * (g + 1)])

    each_head(z, head)
    mix = rows_ref[...]
    rows_out_ref[...] = mix.astype(bf16)
    for c in range(z.nc):
        block_ref[c] = mix[z.rows * c : z.rows * (c + 1)]
    for fy in (0, 1):
        mix_ref[fy] = gathered(z, at, block_ref, fy).astype(bf16)
    square = jnp.zeros((1, t), f32)
    part = slice(z.lane, z.lane + z.qw)
    for (low, fx, fcore), (high, _, _) in zip(pieces_of(pieces, 0), pieces_of(pieces, 1)):
        d = d_of(at, fx, fcore)
        mid = x_ref[d].astype(f32) + tn(low[:, part], mix_ref[0]) + tn(high[:, part], mix_ref[1])
        mid_ref[d] = mid
        square = square + jnp.sum(mid * mid, axis=0, keepdims=True)
    inv = lax.rsqrt(square * (1.0 / z.width) + eps)
    inv_ref[...] = jnp.broadcast_to(inv, inv_ref.shape)
    for k in range(z.nd):
        d = seen(z, at, k)
        n2_ref[k] = (mid_ref[d] * inv * gain_ref[d][:, 1:2]).astype(bf16)


def forward_call(z, small, places, q, x_d, gain_d, chunks, pieces):
    t = z.tokens
    outs = [
        sds((2, z.length * z.rows, t), bf16),
        sds((QH * HD, t), bf16),
        sds((8, GRP * t), f32),
        sds((z.nd, z.qw, t), f32),
        sds((8, t), f32),
        sds((z.nd, z.qw, t), bf16),
    ]
    scratch = [
        pltpu.VMEM((2 * KVW, z.nc * t), bf16),
        pltpu.VMEM((z.nc * t, t), f32),
        pltpu.VMEM((QH * HD, t), f32),
        pltpu.VMEM((z.nc, z.rows, t), f32),
    ]
    args = [small, places, q, x_d, gain_d] + chunks + pieces
    flops = 4 * z.nc * t * t * QH * HD + 2 * t * z.width**2
    return call(forward_kernel, z, outs, args, scratch, flops)


def ffn_act(z, gate, up, act_grad, act_ref, gu_ref):
    u = z.units
    sigma = jax.nn.sigmoid(gate)
    gs = gate * sigma
    act_ref[...] = (gs * up).astype(bf16)
    gu_ref[:u] = (act_grad * up * sigma * (1.0 + gate * (1.0 - sigma))).astype(bf16)
    gu_ref[u:] = (act_grad * gs).astype(bf16)


def give_slots(z, out, d, mine_ref, other_ref):
    t = z.tokens
    for i in range(4):
        mine_ref[i, d] = out[:, t * i : t * (i + 1)].astype(bf16)
        other_ref[i, d] = out[:, t * (4 + i) : t * (5 + i)].astype(bf16)


KEPT = (0, 1, 3, 2)


def ffn_first_kernel(z, *refs):
    t, u, b = z.tokens, z.units, 2 * z.rows
    cots, ws = refs[:8], refs[8:11]
    w_ref, turned_ref, cot_ref, grad_ref = refs[11:]
    at = place()
    for n, k in enumerate(KEPT):
        if n < 3:
            w_ref[b * n : b * (n + 1), :] = ws[n][...]
        for i in range(8):
            cot_ref[b * n : b * (n + 1), t * i : t * (i + 1)] = cots[i][seen(z, at, k)]
    turned_ref[...] = jnp.transpose(w_ref[:, : 2 * u])
    grad_ref[...] = tn(w_ref[:, 2 * u :], cot_ref[: 3 * b, :])


def ffn_kernel(z, w_ref, turned_ref, grad_ref, cot_ref, far_ref, *refs):
    n2s, (mine_ref, other_ref, gu_ref, act_ref, n2_ref) = refs[:8], refs[8:]
    t, u, b = z.tokens, z.units, 2 * z.rows
    at = place()
    for n, k in enumerate(KEPT):
        for i in range(8):
            n2_ref[b * n : b * (n + 1), t * i : t * (i + 1)] = n2s[i][b * k : b * (k + 1), :]
    gate_up = nn(turned_ref[...], n2_ref[: 3 * b, :]) + tn(far_ref[:, : 2 * u], n2_ref[3 * b :, :])
    act_grad = grad_ref[...] + tn(far_ref[:, 2 * u :], cot_ref[3 * b :, :])
    ffn_act(z, gate_up[:u], gate_up[u:], act_grad, act_ref, gu_ref)
    for n, k in enumerate(KEPT):
        w = far_ref[:, : 2 * u] if n == 3 else w_ref[b * n : b * (n + 1), : 2 * u]
        give_slots(z, nn(w, gu_ref[...]), seen(z, at, k), mine_ref, other_ref)


def ffn_blocks_kernel(z, *refs):
    L = z.length
    n2s, cots, gus, dts = refs[:8], refs[8:16], refs[16 : 16 + L], refs[16 + L : 16 + 2 * L]
    mine_ref, other_ref, gu_ref, act_ref, n2_ref, cot_ref, pre_ref, ag_ref, line_ref, part_ref = refs[16 + 2 * L :]
    at = place()
    u, rows = z.units, 2 * z.rows
    t = z.tokens
    for i in range(8):
        n2_ref[:, t * i : t * (i + 1)] = n2s[i][...]
        for d in range(z.nd):
            part_ref[d, :, t * i : t * (i + 1)] = cots[i][d]
            cot_ref[z.qw * d : z.qw * (d + 1), t * i : t * (i + 1)] = cots[i][d]
    for l in range(L):
        line_ref[l] = n2_ref[rows * l : rows * (l + 1), :]
    pre_ref[...] = jnp.zeros_like(pre_ref)
    ag_ref[...] = jnp.zeros_like(ag_ref)
    for k in range(L):
        l = lax.rem(at.l + k, L)
        part, units = down_part(z, l)
        pre_ref[...] += tn(gus[k][...], line_ref[l])
        ag_ref[units, :] += tn(dts[k][...], part_ref[part])
    ffn_act(z, pre_ref[:u], pre_ref[u:], ag_ref[...], act_ref, gu_ref)
    for k in range(L):
        line_ref[lax.rem(at.l + k, L)] = nn(gus[k][...], gu_ref[...]).astype(bf16)
    for d in range(z.nd):
        out = jnp.concatenate([line_ref[z.fold * d + i] for i in range(z.fold)], axis=0)
        give_slots(z, out, d, mine_ref, other_ref)


def ffn_call(z, n2s, cots, gus, dts):
    t, L, u = z.tokens, z.length, z.units
    outs = [
        sds((4, z.nd, z.qw, t), bf16),
        sds((4, z.nd, z.qw, t), bf16),
        sds((2 * u, 8 * t), bf16),
        sds((u, 8 * t), bf16),
        sds((z.width, 8 * t), bf16),
        sds((z.width, 8 * t), bf16),
    ]
    flops = 2 * 8 * t * z.width * 5 * u
    if z.fold == 1:
        firsts = [
            sds((6 * z.rows, 3 * u), bf16),
            sds((2 * u, 6 * z.rows), bf16),
            outs[5],
            sds((u, 8 * t), f32),
        ]
        near = [gus[k] for k in KEPT[:3]]
        w, turned, cot, grad = call(ffn_first_kernel, z, firsts, cots + near, (), flops // 5)
        args = [w, turned, grad, cot, gus[KEPT[3]]] + n2s
        return list(call(ffn_kernel, z, outs[:5], args, (), flops)) + [cot]
    scratch = [
        pltpu.VMEM((2 * u, 8 * t), f32),
        pltpu.VMEM((u, 8 * t), f32),
        pltpu.VMEM((L, 2 * z.rows, 8 * t), bf16),
        pltpu.VMEM((z.nd, z.qw, 8 * t), bf16),
    ]
    return call(ffn_blocks_kernel, z, outs, n2s + cots + gus + dts, scratch, flops)


def down_part(z, l):
    i = lax.rem(l, z.fold)
    rows = slice(None) if z.fold == 1 else pl.ds(pl.multiple_of(i * z.down_rows, z.down_rows), z.down_rows)
    return l // z.fold, rows


def hidden_kernel(z, act_ref, *refs):
    L, u = z.length, z.units
    dts, (mine_ref, other_ref, sum_ref) = refs[:L], refs[L:]
    at = place()
    if z.fold == 1:
        for k in range(L):
            give_slots(z, nn(dts[k][:, 2 * u :], act_ref[...]), seen(z, at, k), mine_ref, other_ref)
    else:
        sum_ref[...] = jnp.zeros_like(sum_ref)
        for k in range(L):
            part, units = down_part(z, lax.rem(at.l + k, L))
            sum_ref[part] += nn(dts[k][...], act_ref[units, :])
        for d in range(z.nd):
            give_slots(z, sum_ref[d], d, mine_ref, other_ref)


def hidden_call(z, act, dts):
    t = z.tokens
    outs = [sds((4, z.nd, z.qw, t), bf16)] * 2
    scratch = [pltpu.VMEM((z.nd, z.qw, 8 * t) if z.fold != 1 else (8, 128), f32)]
    return call(hidden_kernel, z, outs, [act] + dts, scratch, 16 * t * z.width * z.units)


def ffn_weights_kernel(z, gu_ref, act_ref, n2_ref, cot_ref, *refs):
    L, u = z.length, z.units
    at = place()
    for n in range(L):
        k = KEPT[n] if z.fold == 1 else n
        rows = slice(2 * z.rows * n, 2 * z.rows * (n + 1))
        if z.fold == 1:
            refs[k][:, : 2 * u] = nt(n2_ref[rows, :], gu_ref[...]).astype(bf16)
            refs[k][:, 2 * u :] = nt(cot_ref[rows, :], act_ref[...]).astype(bf16)
        else:
            refs[2 * L][k] = nt(n2_ref[rows, :], gu_ref[...]).astype(bf16)
    if z.fold != 1:
        for d in range(z.nd):
            down = nt(cot_ref[z.qw * d : z.qw * (d + 1), :], act_ref[...])
            for i in range(z.fold):
                block = down[:, z.down_rows * i : z.down_rows * (i + 1)]
                refs[2 * L + 1][z.fold * d + i] = block.astype(bf16)
        for k in range(L):
            l = lax.rem(at.l + k, L)
            refs[k][...] = refs[2 * L][l]
            refs[L + k][...] = refs[2 * L + 1][l]


def ffn_weights_call(z, gu, act, n2, cot):
    L, scratch = z.length, []
    if z.fold == 1:
        outs = [sds((2 * z.rows, 3 * z.units), bf16)] * L
    else:
        shapes = (2 * z.rows, 2 * z.units), (z.qw, z.down_rows)
        outs = [sds(shape, bf16) for shape in shapes for _ in range(L)]
        scratch = [pltpu.VMEM((L,) + shape, bf16) for shape in shapes]
    flops = 2 * 8 * z.tokens * z.width * 3 * z.units
    out = call(ffn_weights_kernel, z, outs, [gu, act, n2, cot], scratch, flops)
    return out[:L], out[L:]


def core_sum(mine, got):
    total = [mine[i].astype(f32) + got[i].astype(f32) for i in range(4)]
    return [total[0]] + [part.astype(bf16) for part in total[1:]]


def slab_sum(z, own, got):
    out = []
    for k in range(z.length):
        n = own.shape[0] // z.length
        part = k if own.ndim == 3 else slice(n * k, n * (k + 1))
        total = own[part]
        for g in got:
            total = total + g[part].astype(f32)
        out.append(total if k == 0 else total.astype(bf16))
    return out


def backward_kernel(z, small_ref, places_ref, q_ref, mid_ref, inv_ref, gain_ref, cot_ref, mix_ref, lse_ref, cos_ref, sin_ref, own_ref, *refs):
    n = z.nc
    got, refs = refs[:3], refs[3:]
    chunks, pieces = refs[:n], refs[n : n + 8]
    midg_ref, midb_ref, gain_two_ref, dq_ref, *dkv_refs = refs[n + 8 : 2 * n + 12]
    kv_ref, bias_ref, grad_ref, dk_ref, rows_ref, dq_rows_ref = refs[2 * n + 12 :]
    at = place()
    t = z.tokens
    inv = inv_ref[0:1, :]
    mean = jnp.zeros((1, t), f32)
    for d in range(z.nd):
        g = own_ref[d] + got[0][d].astype(f32) + got[1][d].astype(f32) + got[2][d].astype(f32)
        mid = mid_ref[d]
        gain_two_ref[d] = jnp.broadcast_to(jnp.sum(g * mid * inv, axis=1, keepdims=True), (z.qw, 8))
        u = g * gain_ref[d][:, 1:2]
        midg_ref[d] = u
        mean = mean + jnp.sum(u * mid, axis=0, keepdims=True)
    scale = inv * inv * mean * (1.0 / z.width)
    for d in range(z.nd):
        full = cot_ref[d].astype(f32) + inv * (midg_ref[d] - mid_ref[d] * scale)
        midg_ref[d] = full
        midb_ref[d] = full.astype(bf16)
    part = slice(z.lane, z.lane + z.qw)
    for fy in (0, 1):
        acc = jnp.zeros((z.length * z.rows, t), f32)
        for piece, fx, fcore in pieces_of(pieces, fy):
            acc = acc + nn(piece[:, part], midb_ref[d_of(at, fx, fcore)])
        for k in range(z.length):
            grad_ref[c_of(z, at, fy, k)] = acc[z.rows * k : z.rows * (k + 1)]
    lay_keys(z, at, chunks, small_ref, places_ref, kv_ref, bias_ref)
    rows_ref[...] = jnp.concatenate([grad_ref[c] for c in range(z.nc)], axis=0)
    cos, sin = cos_ref[...], sin_ref[...]
    factor = HD**-0.5

    def head(h):
        q3 = three(q_ref, h)
        g3 = three(rows_ref, h).astype(bf16)
        delta = jnp.sum(g3.astype(f32) * three(mix_ref, h).astype(f32), axis=0, keepdims=True)
        key, value = head_of(kv_ref, h), head_of(kv_ref, KVH + h)
        p = jnp.exp(scores(kv_ref, bias_ref, h, q3) - lse_ref[pl.ds(h, 1), :])
        dv = nt(g3, p.astype(bf16))
        ds = (p * (tn(value, g3) - delta)).astype(bf16)
        dk = nt(q3, ds) * factor
        dq = nn(key, ds) * factor
        put_head(dk_ref, h, dk.astype(bf16))
        put_head(dk_ref, KVH + h, dv.astype(bf16))
        for g in range(GRP):
            put_head(dq_rows_ref, GRP * h + g, dq[:, t * g : t * (g + 1)])

    each_head(z, head)
    rows = rotate(dq_rows_ref[...], cos, -sin)
    for d in range(z.nd):
        dq_ref[d] = rows[z.qw * d : z.qw * (d + 1)].astype(bf16)
    for i, out in enumerate(dkv_refs):
        out[...] = dk_ref[:, t * i : t * (i + 1)]


def backward_call(z, small, places, q, mid, inv, gain_d, cot_d, mix, lse, cos, sin, own, got, chunks, pieces):
    t = z.tokens
    outs = [
        sds((z.nd, z.qw, t), f32),
        sds((z.nd, z.qw, t), bf16),
        sds((z.nd, z.qw, 8), f32),
        sds((z.nd, z.qw, t), bf16),
    ] + [sds((2 * KVW, t), bf16)] * z.nc
    scratch = [
        pltpu.VMEM((2 * KVW, z.nc * t), bf16),
        pltpu.VMEM((z.nc * t, t), f32),
        pltpu.VMEM((z.nc, z.rows, t), f32),
        pltpu.VMEM((2 * KVW, z.nc * t), bf16),
    ] + [pltpu.VMEM((QH * HD, t), f32)] * 2
    args = [small, places, q, mid, inv, gain_d, cot_d, mix, lse, cos, sin, own] + list(got) + chunks + pieces
    flops = 10 * z.nc * t * t * QH * HD + 2 * t * z.width**2
    return call(backward_kernel, z, outs, args, scratch, flops)


def qo_weights_kernel(z, n1_ref, mix_ref, dq_ref, midb_ref, gain_two_ref, *refs):
    pieces, (mine_ref, other_ref, nog_ref) = refs[:8], refs[8:]
    at = place()
    fill = jnp.zeros((z.length * z.rows, z.lane - z.qw - 8), f32)
    for fy in (0, 1):
        gain = jnp.concatenate([gathered(z, at, gain_two_ref, fy), fill], axis=1)
        acc = jnp.zeros((z.length * z.rows, z.tokens), f32)
        for piece, fx, fcore in pieces_of(pieces, fy)[::-1]:
            d, out = d_of(at, fx, fcore), other_ref if fcore else mine_ref
            block = jnp.concatenate([nt(n1_ref[fy], dq_ref[d]), gain], axis=1)
            out[fx + 2 * fy, :, : z.lane] = block.astype(bf16)
            out[fx + 2 * fy, :, z.lane :] = nt(mix_ref[fy], midb_ref[d]).astype(bf16)
            acc = acc + nn(piece[:, : z.qw], dq_ref[d])
        nog_ref[fy] = acc


def qo_weights_call(z, n1, mix, dq, midb, gain_two, pieces):
    blocks = (4, z.length * z.rows, z.lane + z.qw)
    outs = [sds(blocks, bf16), sds(blocks, bf16), sds(n1.shape, f32)]
    args = [n1, mix, dq, midb, gain_two] + pieces
    return call(qo_weights_kernel, z, outs, args, (), 6 * z.tokens * z.width**2)


def end_kernel(z, x_ref, inv_ref, gain_ref, n1_ref, midg_ref, nog_ref, cos_ref, sin_ref, own_ref, *refs):
    got, refs = refs[: z.length], refs[z.length :]
    pieces, (grad_ref, mine_ref, other_ref, dkv_ref, u_ref) = refs[:8], refs[8:]
    at = place()
    t, w = z.tokens, 2 * z.kw
    total = own_ref[...].astype(f32)
    for g in got:
        total = total + g[...].astype(f32)
    dk = rotate(total[:KVW], cos_ref[...], -sin_ref[...])
    for d in range(z.nd):
        dkv_ref[d, : z.kw] = dk[z.kw * d : z.kw * (d + 1)].astype(bf16)
        dkv_ref[d, z.kw :] = total[KVW + z.kw * d : KVW + z.kw * (d + 1)].astype(bf16)
    inv = inv_ref[0:1, :]
    mean = jnp.zeros((1, t), f32)
    columns = [(fx, fcore) for _, fx, fcore in pieces_of(pieces, 0)]
    every = jnp.concatenate([dkv_ref[d_of(at, fx, fcore)] for fx, fcore in columns], axis=0)
    for fy in (0, 1):
        nog = nog_ref[fy]
        for k in range(z.length):
            c = c_of(z, at, fy, k)
            block = slice(z.rows * k, z.rows * (k + 1))
            weights = jnp.concatenate([p[k, :w, :] for p, _, _ in pieces_of(pieces, fy)], axis=0)
            acc = nog[block] + tn(weights, every)
            x = x_ref[c].astype(f32)
            row = jnp.sum(jnp.transpose(acc * x * inv), axis=0, keepdims=True)
            gain = jnp.broadcast_to(row, (8, z.rows)).astype(bf16)
            u = acc * gain_ref[c][:, 0:1]
            u_ref[c] = u
            mean = mean + jnp.sum(u * x, axis=0, keepdims=True)
            terms = nt(every, n1_ref[fy][block]).astype(bf16)
            for i, (fx, fcore) in enumerate(columns):
                out = other_ref if fcore else mine_ref
                out[fx + 2 * fy, k, :w] = terms[w * i : w * (i + 1)]
                out[fx + 2 * fy, k, w : w + 8] = gain
    scale = inv * inv * mean * (1.0 / z.width)
    for c in range(z.nc):
        x = x_ref[c].astype(f32)
        grad_ref[c] = midg_ref[c] + inv * (u_ref[c] - x * scale)


def end_call(z, x_c, inv, gain, n1, midg_c, nog, cos, sin, own, got, pieces):
    t = z.tokens
    blocks = (4, z.length, 2 * z.kw + 8, z.rows)
    outs = [sds((z.nc, z.rows, t), f32), sds(blocks, bf16), sds(blocks, bf16)]
    scratch = [pltpu.VMEM((z.nd, 2 * z.kw, t), bf16), pltpu.VMEM((z.nc, z.rows, t), f32)]
    args = [x_c, inv, gain, n1, midg_c, nog, cos, sin, own] + got + pieces
    return call(end_kernel, z, outs, args, scratch, 8 * t * z.width * KVW)


def layer(
    nd, nc, hidden_in, positions, attn_gain, query_w, key_w, value_w, output_w,
    ffn_gain, gate_w, up_w, down_w, cotangent,
):
    _, tokens, width = hidden_in.shape
    z = SimpleNamespace(nd=nd, nc=nc, length=nc // 2, tokens=tokens, width=width, rows=width // nc)
    z.qw, z.kw, z.units = query_w.shape[1], key_w.shape[1], gate_w.shape[1] // 2
    z.down_rows, z.fold = down_w.shape[0], nc // (2 * nd)
    z.lane = -(-(z.qw + 8) // 128) * 128
    z.dt_lane = 2 * z.units if z.fold == 1 else 0
    L, t, rows = z.length, tokens, z.rows
    grad_scale = float(tokens * nd * nc) ** (-0.5)
    y0 = lax.rem(lax.axis_index("ctx"), 2)

    x_t, cot_t = hidden_in[0].T, cotangent[0].T
    x_c, x_d, cot_d = x_t.reshape(nc, rows, t), x_t.reshape(nd, z.qw, t), cot_t.reshape(nd, z.qw, t)

    def along_line(x):
        return [x] + [from_line(z, x, k) for k in range(1, L)]

    def over_slab(x, relay=False):
        mine = [x] + [to_slot(z, x, i) for i in (1, 2)]
        if relay:
            mine += [to_slot(z, mine[2], 1)]
        else:
            mine += [to_slot(z, x, 3)]
        return mine + [to_core(z, p) for p in mine]

    def flat(x):
        return x.reshape((L * x.shape[1],) + x.shape[2:])

    kv_line = along_line(first_call(z, key_w.T, value_w.T, attn_gain, ffn_gain, positions))
    kv_w = over_slab(jnp.stack(kv_line))

    pad = z.lane - z.qw
    qo = jnp.concatenate([jnp.pad(query_w, ((0, 0), (0, pad))), output_w], axis=1)
    qo_line = along_line(qo)
    qo_w = over_slab(flat(jnp.stack(qo_line)), relay=True)

    def own_half(w, other):
        low = (y0 == 0) != other
        return jnp.where(low, w[:, : z.units], w[:, z.units :])

    keep = jnp.concatenate([own_half(gate_w, False), own_half(up_w, False)], axis=1)
    give = jnp.concatenate([own_half(gate_w, True), own_half(up_w, True)], axis=1)
    take = to_slot(z, give, 2)
    gate_up = jnp.where(
        y0 == 0, jnp.concatenate([keep, take], axis=0), jnp.concatenate([take, keep], axis=0)
    )

    def down_target(d, c):
        n, i = c // z.fold, c % z.fold
        return n // 2, 2 * (z.fold * d + i) + n % 2

    down_back = {down_target(d, c): (d, c) for d in range(nd) for c in range(nc)}
    down_t = moved(z, down_w.T, down_target)
    if z.fold == 1:
        gus = line_pieces(z, jnp.concatenate([gate_up, down_t], axis=1))
        dts = gus
    else:
        gus, dts = line_pieces(z, gate_up), line_pieces(z, down_t)

    frequency = jnp.power(rope_base, -2.0 * jnp.arange(HALF, dtype=f32) / HD)
    angles = frequency[:, None] * positions[0].astype(f32)[None, :]
    cos, sin = jnp.cos(angles), jnp.sin(angles)
    places = jnp.broadcast_to(positions[0].astype(f32)[None, :], (8, t))

    kv, n1, inv_one, gain, small = kv_call(z, x_c, cos, sin, kv_w)
    gain_d = gain.reshape(nd, z.qw, 8)
    kv_along = along_line(kv)
    chunks = kv_along + [to_slot(z, p, 2) for p in kv_along]
    q = q_call(z, n1, cos, sin, qo_w)
    mix, mix_rows, lse, mid, inv_two, n2 = forward_call(z, small, places, q, x_d, gain_d, chunks, qo_w)

    cots = over_slab(cot_d, relay=True)
    n2s = over_slab(n2.reshape(width, t))
    ntg_mine, ntg_other, gu, act, n2_all, cot_all = ffn_call(z, n2s, cots, gus, dts)
    ntg_own, *ntg_send = core_sum(ntg_mine, to_core(z, ntg_other))
    ntg_got = [to_slot(z, s, i + 1) for i, s in enumerate(ntg_send)]

    hid_mine, hid_other = hidden_call(z, act, dts)
    hid_own, *hid_send = core_sum(hid_mine, to_core(z, hid_other))
    gu_grads, dt_grads = ffn_weights_call(z, gu, act, n2_all, cot_all)

    midg, midb, gain_two, dq, *dkv = backward_call(
        z, small, places, q, mid, inv_two, gain_d, cot_d, mix_rows, lse, cos, sin,
        ntg_own, ntg_got, chunks, qo_w,
    )

    dkv_got = []
    for k in range(L):
        got = to_slot(z, dkv[L + k], 2)
        if k == 0:
            dkv_got.append(got)
        else:
            both = (dkv[k].astype(f32) + got.astype(f32)).astype(bf16)
            dkv_got.append(from_line(z, both, -k))

    qo_mine, qo_other, nog = qo_weights_call(
        z, n1, mix, dq, midb, gain_two.reshape(nc, rows, 8), qo_w
    )
    grad_in, kv_mine, kv_other = end_call(
        z, x_c, inv_one, gain, n1, midg.reshape(nc, rows, t), nog, cos, sin, dkv[0], dkv_got, kv_w
    )

    def to_owner(mine, other):
        own, *sends = core_sum(mine, to_core(z, other))
        got = [to_slot(z, s, i + 1) for i, s in enumerate(sends)]
        return line_sum(slab_sum(z, own, got))

    def line_sum(pieces):
        total = pieces[0].astype(f32)
        for k in range(1, L):
            total = total + from_line(z, pieces[k], -k).astype(f32)
        return total * grad_scale

    sum_kv = to_owner(kv_mine, kv_other)
    sum_qo = to_owner(qo_mine, qo_other)

    hidden_out = mid + hid_own
    for i, s in enumerate(hid_send):
        hidden_out = hidden_out + to_slot(z, s, i + 1).astype(f32)

    s_gu = line_sum(gu_grads)
    s_dt = s_gu[:, 2 * z.units :] if z.fold == 1 else line_sum(dt_grads)
    s_gu = s_gu[:, : 2 * z.units]
    mine = jnp.where(y0 == 0, s_gu[:rows], s_gu[rows:])
    theirs = jnp.where(y0 == 0, s_gu[rows:], s_gu[:rows]).astype(bf16)
    theirs = to_slot(z, theirs, 2).astype(f32)
    low, high = jnp.where(y0 == 0, mine, theirs), jnp.where(y0 == 0, theirs, mine)
    grad_gate = jnp.concatenate([low[:, : z.units], high[:, : z.units]], axis=1)
    grad_up = jnp.concatenate([low[:, z.units :], high[:, z.units :]], axis=1)
    s_dt = moved(z, s_dt.astype(bf16), lambda d, c: down_back[(d, c)])
    grad_down = s_dt.astype(f32).T

    kw, qw, w = z.kw, z.qw, 2 * z.kw
    return (
        hidden_out.reshape(width, t).T[None],
        grad_in.reshape(width, t).T[None],
        sum_kv[w],
        sum_qo[:, :qw],
        sum_kv[:kw].T,
        sum_kv[kw:w].T,
        sum_qo[:, z.lane :],
        sum_qo[:, qw],
        grad_gate,
        grad_up,
        grad_down,
    )


def solution(mesh):
    nd, nc = mesh.shape["dp"], mesh.shape["ctx"]
    whole, rows, gain = P("dp", "ctx", None), P("ctx", "dp"), P("ctx")
    in_specs = (whole, P("dp", "ctx"), gain, rows, rows, rows, rows, gain, rows, rows, rows, whole)
    out_specs = (whole, whole, gain, rows, rows, rows, rows, gain, rows, rows, rows)
    return jax.shard_map(
        functools.partial(layer, nd, nc),
        mesh=mesh,
        in_specs=in_specs,
        out_specs=out_specs,
        check_vma=False,
    )
```

```python
import functools
from types import SimpleNamespace

import jax
import jax.numpy as jnp
from jax import lax
from jax.experimental import pallas as pl
from jax.experimental.pallas import tpu as pltpu
from jax.sharding import PartitionSpec as P


QH = 15
KVH = 5
HD = 64
HALF = HD // 2
GRP = QH // KVH
KVW = KVH * HD
eps = 1e-05
rope_base = 10000.0
neg_big = -1e30
AX = ("dp", "ctx")
f32 = jnp.float32
bf16 = jnp.bfloat16


SLOTS = ((0, 0), (1, 0), (0, 1), (1, 1))


def moved(z, x, target):
    table = []
    for d in range(z.nd):
        for c in range(z.nc):
            dd, cc = target(d, c)
            table.append((d * z.nc + c, dd * z.nc + cc))
    return lax.ppermute(x, AX, table)


def to_slot(z, x, i):
    fx, fy = SLOTS[i]
    return moved(z, x, lambda d, c: (d ^ (2 * fx), c ^ fy))


def to_core(z, x):
    return moved(z, x, lambda d, c: (d ^ 1, c))


def from_line(z, x, k):
    k = k % z.length
    return moved(z, x, lambda d, c: (d, 2 * ((c // 2 - k) % z.length) + c % 2))


def line_pieces(z, x):
    if z.length != 4:
        return [x] + [from_line(z, x, k) for k in range(1, z.length)]
    one, three = from_line(z, x, 1), from_line(z, x, 3)
    return [x, one, from_line(z, one, 1), three]


def nt(a, b):
    return lax.dot_general(a, b, (((1,), (1,)), ((), ())), preferred_element_type=f32)


def nn(a, b):
    return lax.dot_general(a, b, (((1,), (0,)), ((), ())), preferred_element_type=f32)


def tn(a, b):
    return lax.dot_general(a, b, (((0,), (0,)), ((), ())), preferred_element_type=f32)


def place():
    d0, c0 = lax.axis_index("dp"), lax.axis_index("ctx")
    return SimpleNamespace(x=d0 // 2, core=lax.rem(d0, 2), l=c0 // 2, y=lax.rem(c0, 2))


def flip(bit, f):
    return 1 - bit if f else bit


def d_of(at, fx, fcore):
    return 2 * flip(at.x, fx) + flip(at.core, fcore)


def c_of(z, at, fy, k):
    return 2 * lax.rem(at.l + k, z.length) + flip(at.y, fy)


def pieces_of(pieces, fy):
    return [(pieces[4 * fcore + fx + 2 * fy], fx, fcore) for fcore in (0, 1) for fx in (0, 1)]


def gathered(z, at, ref, fy):
    return jnp.concatenate([ref[c_of(z, at, fy, k)] for k in range(z.length)], axis=0)


def seen(z, at, k):
    return lax.rem(at.l + k, z.nd) if z.fold == 1 else k


VM = pl.BlockSpec(memory_space=pltpu.VMEM)


def call(kernel, z, outs, args, scratch=(), flops=0):
    moved_bytes = sum(a.size * a.dtype.itemsize for a in args)
    moved_bytes += sum(o.size * o.dtype.itemsize for o in outs)
    return pl.pallas_call(
        functools.partial(kernel, z),
        out_shape=tuple(outs),
        in_specs=[VM] * len(args),
        out_specs=tuple([VM] * len(outs)),
        scratch_shapes=list(scratch),
        compiler_params=pltpu.CompilerParams(vmem_limit_bytes=56 << 20),
        cost_estimate=pl.CostEstimate(
            flops=int(flops), transcendentals=0, bytes_accessed=int(moved_bytes)
        ),
    )(*args)


def sds(shape, dtype):
    return jax.ShapeDtypeStruct(shape, dtype)


def rotate(rows, cos, sin):
    out = []
    for i in range(rows.shape[0] // HD):
        a, b = rows[HD * i : HD * i + HALF], rows[HD * i + HALF : HD * (i + 1)]
        out += [a * cos - b * sin, b * cos + a * sin]
    return jnp.concatenate(out, axis=0)


def first_kernel(z, key_ref, value_ref, gain_one_ref, gain_two_ref, places_ref, out_ref):
    half = z.tokens // 2
    blocks = [places_ref[0:1, half * i : half * i + 1].astype(f32) * (1.0 / half) for i in (0, 1)]
    rows = [gain_one_ref[...].astype(f32), gain_two_ref[...].astype(f32)]
    rows += [jnp.broadcast_to(b, (1, z.rows)) for b in blocks]
    rows += [jnp.zeros((4, z.rows), f32)]
    out_ref[: z.kw] = key_ref[...]
    out_ref[z.kw : 2 * z.kw] = value_ref[...]
    out_ref[2 * z.kw :] = jnp.concatenate(rows, axis=0).astype(bf16)


def first_call(z, key, value, gain_one, gain_two, places):
    outs = [sds((2 * z.kw + 8, z.rows), bf16)]
    args = [key, value, gain_one[None], gain_two[None], places]
    return call(first_kernel, z, outs, args)[0]


def kv_kernel(z, x_ref, cos_ref, sin_ref, *refs):
    pieces, (kv_ref, n1_ref, inv_ref, gain_ref, small_ref, acc_ref, sum_ref) = refs[:8], refs[8:]
    at = place()
    x = x_ref[...].astype(f32)
    mean = jnp.sum(jnp.sum(x * x, axis=0), axis=0, keepdims=True) * (1.0 / z.width)
    inv = lax.rsqrt(mean + eps)
    inv_ref[...] = jnp.broadcast_to(inv, inv_ref.shape)
    w = 2 * z.kw
    for fy, n in ((0, 0), (1, 2)):
        blocks = []
        for k in range(z.length):
            c = c_of(z, at, fy, k)
            small = pieces[n][k, w : w + 8, :].astype(f32)
            small_ref[c] = small
            gain = jnp.transpose(small)
            gain_ref[c] = gain
            block = x_ref[c].astype(f32) * inv * gain[:, 0:1]
            blocks.append(block)
            weights = jnp.concatenate([p[k, :w, :] for p, _, _ in pieces_of(pieces, fy)], axis=0)
            out = nn(weights, block.astype(bf16))
            if fy == 0 and k == 0:
                sum_ref[...] = out
            else:
                sum_ref[...] += out
        n1_ref[fy] = jnp.concatenate(blocks, axis=0).astype(bf16)
    for i, (_, fx, fcore) in enumerate(pieces_of(pieces, 0)):
        acc_ref[d_of(at, fx, fcore)] = sum_ref[w * i : w * (i + 1)]
    key = jnp.concatenate([acc_ref[d, : z.kw] for d in range(z.nd)], axis=0)
    value = jnp.concatenate([acc_ref[d, z.kw :] for d in range(z.nd)], axis=0)
    kv_ref[:KVW] = rotate(key, cos_ref[...], sin_ref[...]).astype(bf16)
    kv_ref[KVW:] = value.astype(bf16)


def kv_call(z, x_c, cos, sin, pieces):
    t = z.tokens
    outs = [
        sds((2 * KVW, t), bf16),
        sds((2, z.length * z.rows, t), bf16),
        sds((8, t), f32),
        sds((z.nc, z.rows, 8), f32),
        sds((z.nc, 8, z.rows), f32),
    ]
    scratch = [pltpu.VMEM((z.nd, 2 * z.kw, t), f32), pltpu.VMEM((z.nd * 2 * z.kw, t), f32)]
    return call(kv_kernel, z, outs, [x_c, cos, sin] + pieces, scratch, 2 * t * z.width * 2 * KVW)


def q_kernel(z, n1_ref, cos_ref, sin_ref, *refs):
    pieces, (q_ref, acc_ref) = refs[:8], refs[8:]
    at = place()
    for (low, fx, fcore), (high, _, _) in zip(pieces_of(pieces, 0), pieces_of(pieces, 1)):
        out = tn(low[:, : z.qw], n1_ref[0]) + tn(high[:, : z.qw], n1_ref[1])
        acc_ref[d_of(at, fx, fcore)] = out
    q = jnp.concatenate([acc_ref[d] for d in range(z.nd)], axis=0)
    q_ref[...] = rotate(q, cos_ref[...], sin_ref[...]).astype(bf16)


def q_call(z, n1, cos, sin, pieces):
    scratch = [pltpu.VMEM((z.nd, z.qw, z.tokens), f32)]
    outs = [sds((QH * HD, z.tokens), bf16)]
    return call(q_kernel, z, outs, [n1, cos, sin] + pieces, scratch, 2 * z.tokens * z.width**2)[0]


def lay_keys(z, at, chunks, small_ref, places_ref, kv_ref, bias_ref):
    t = z.tokens
    row = lax.broadcasted_iota(jnp.int32, (t, t), 0)
    low = row < t // 2
    within = jnp.where(low, row, row - t // 2).astype(f32)
    places = places_ref[0:1, :].astype(f32)
    for n, chunk in enumerate(chunks):
        kv_ref[:, t * n : t * (n + 1)] = chunk[...]
        c = c_of(z, at, n // z.length, n % z.length)
        small = small_ref[c]
        start = jnp.where(low, small[2:3, 0:1], small[3:4, 0:1]) * float(t // 2)
        bias_ref[t * n : t * (n + 1), :] = jnp.where(start + within <= places, 0.0, neg_big)


def three(ref, h):
    return jnp.concatenate([head_of(ref, GRP * h + g) for g in range(GRP)], axis=1)


def scores(kv_ref, bias_ref, h, q3):
    s = tn(head_of(kv_ref, h), q3) * (HD**-0.5)
    bias = bias_ref[...]
    return s + jnp.concatenate([bias] * GRP, axis=1)


def each_head(z, body):
    if z.nc <= 8:
        for h in range(KVH):
            body(h)
    else:
        lax.fori_loop(0, KVH, lambda h, carry: (body(h), carry)[1], 0)


def head_of(ref, n):
    start = HD * n
    return ref[pl.ds(start if isinstance(n, int) else pl.multiple_of(start, HD), HD), :]


def put_head(ref, n, x):
    start = HD * n
    ref[pl.ds(start if isinstance(n, int) else pl.multiple_of(start, HD), HD), :] = x


def forward_kernel(z, small_ref, places_ref, q_ref, x_ref, gain_ref, *refs):
    n = z.nc
    chunks, pieces = refs[:n], refs[n : n + 8]
    mix_ref, rows_out_ref, lse_ref, mid_ref, inv_ref, n2_ref = refs[n + 8 : n + 14]
    kv_ref, bias_ref, rows_ref, block_ref = refs[n + 14 :]
    at = place()
    t = z.tokens
    lay_keys(z, at, chunks, small_ref, places_ref, kv_ref, bias_ref)

    def head(h):
        s = scores(kv_ref, bias_ref, h, three(q_ref, h))
        top = jnp.max(s, axis=0, keepdims=True)
        e = jnp.exp(s - top)
        total = jnp.sum(e, axis=0, keepdims=True)
        lse_ref[pl.ds(h, 1), :] = top + jnp.log(total)
        p = (e * (1.0 / total)).astype(bf16)
        out = nn(head_of(kv_ref, KVH + h), p)
        for g in range(GRP):
            put_head(rows_ref, GRP * h + g, out[:, t * g : t * (g + 1)])

    each_head(z, head)
    mix = rows_ref[...]
    rows_out_ref[...] = mix.astype(bf16)
    for c in range(z.nc):
        block_ref[c] = mix[z.rows * c : z.rows * (c + 1)]
    for fy in (0, 1):
        mix_ref[fy] = gathered(z, at, block_ref, fy).astype(bf16)
    square = jnp.zeros((1, t), f32)
    part = slice(z.lane, z.lane + z.qw)
    for (low, fx, fcore), (high, _, _) in zip(pieces_of(pieces, 0), pieces_of(pieces, 1)):
        d = d_of(at, fx, fcore)
        mid = x_ref[d].astype(f32) + tn(low[:, part], mix_ref[0]) + tn(high[:, part], mix_ref[1])
        mid_ref[d] = mid
        square = square + jnp.sum(mid * mid, axis=0, keepdims=True)
    inv = lax.rsqrt(square * (1.0 / z.width) + eps)
    inv_ref[...] = jnp.broadcast_to(inv, inv_ref.shape)
    for k in range(z.nd):
        d = seen(z, at, k)
        n2_ref[k] = (mid_ref[d] * inv * gain_ref[d][:, 1:2]).astype(bf16)


def forward_call(z, small, places, q, x_d, gain_d, chunks, pieces):
    t = z.tokens
    outs = [
        sds((2, z.length * z.rows, t), bf16),
        sds((QH * HD, t), bf16),
        sds((8, GRP * t), f32),
        sds((z.nd, z.qw, t), f32),
        sds((8, t), f32),
        sds((z.nd, z.qw, t), bf16),
    ]
    scratch = [
        pltpu.VMEM((2 * KVW, z.nc * t), bf16),
        pltpu.VMEM((z.nc * t, t), f32),
        pltpu.VMEM((QH * HD, t), f32),
        pltpu.VMEM((z.nc, z.rows, t), f32),
    ]
    args = [small, places, q, x_d, gain_d] + chunks + pieces
    flops = 4 * z.nc * t * t * QH * HD + 2 * t * z.width**2
    return call(forward_kernel, z, outs, args, scratch, flops)


def ffn_act(z, gate, up, act_grad, act_ref, gu_ref):
    u = z.units
    sigma = jax.nn.sigmoid(gate)
    gs = gate * sigma
    act_ref[...] = (gs * up).astype(bf16)
    gu_ref[:u] = (act_grad * up * sigma * (1.0 + gate * (1.0 - sigma))).astype(bf16)
    gu_ref[u:] = (act_grad * gs).astype(bf16)


def give_slots(z, out, d, mine_ref, other_ref):
    t = z.tokens
    for i in range(4):
        mine_ref[i, d] = out[:, t * i : t * (i + 1)].astype(bf16)
        other_ref[i, d] = out[:, t * (4 + i) : t * (5 + i)].astype(bf16)


KEPT = (0, 1, 3, 2)


def ffn_first_kernel(z, *refs):
    t, u, b = z.tokens, z.units, 2 * z.rows
    cots, ws = refs[:8], refs[8:11]
    w_ref, turned_ref, cot_ref, grad_ref = refs[11:]
    at = place()
    for n, k in enumerate(KEPT):
        if n < 3:
            w_ref[b * n : b * (n + 1), :] = ws[n][...]
        for i in range(8):
            cot_ref[b * n : b * (n + 1), t * i : t * (i + 1)] = cots[i][seen(z, at, k)]
    turned_ref[...] = jnp.transpose(w_ref[:, : 2 * u])
    grad_ref[...] = tn(w_ref[:, 2 * u :], cot_ref[: 3 * b, :])


def ffn_kernel(z, w_ref, turned_ref, grad_ref, cot_ref, far_ref, *refs):
    n2s, (mine_ref, other_ref, gu_ref, act_ref, n2_ref) = refs[:8], refs[8:]
    t, u, b = z.tokens, z.units, 2 * z.rows
    at = place()
    for n, k in enumerate(KEPT):
        for i in range(8):
            n2_ref[b * n : b * (n + 1), t * i : t * (i + 1)] = n2s[i][b * k : b * (k + 1), :]
    gate_up = nn(turned_ref[...], n2_ref[: 3 * b, :]) + tn(far_ref[:, : 2 * u], n2_ref[3 * b :, :])
    act_grad = grad_ref[...] + tn(far_ref[:, 2 * u :], cot_ref[3 * b :, :])
    ffn_act(z, gate_up[:u], gate_up[u:], act_grad, act_ref, gu_ref)
    for n, k in enumerate(KEPT):
        w = far_ref[:, : 2 * u] if n == 3 else w_ref[b * n : b * (n + 1), : 2 * u]
        give_slots(z, nn(w, gu_ref[...]), seen(z, at, k), mine_ref, other_ref)


def ffn_blocks_kernel(z, *refs):
    L = z.length
    n2s, cots, gus, dts = refs[:8], refs[8:16], refs[16 : 16 + L], refs[16 + L : 16 + 2 * L]
    mine_ref, other_ref, gu_ref, act_ref, n2_ref, cot_ref, pre_ref, ag_ref, line_ref, part_ref = refs[16 + 2 * L :]
    at = place()
    u, rows = z.units, 2 * z.rows
    t = z.tokens
    for i in range(8):
        n2_ref[:, t * i : t * (i + 1)] = n2s[i][...]
        for d in range(z.nd):
            part_ref[d, :, t * i : t * (i + 1)] = cots[i][d]
            cot_ref[z.qw * d : z.qw * (d + 1), t * i : t * (i + 1)] = cots[i][d]
    for l in range(L):
        line_ref[l] = n2_ref[rows * l : rows * (l + 1), :]
    pre_ref[...] = jnp.zeros_like(pre_ref)
    ag_ref[...] = jnp.zeros_like(ag_ref)
    for k in range(L):
        l = lax.rem(at.l + k, L)
        part, units = down_part(z, l)
        pre_ref[...] += tn(gus[k][...], line_ref[l])
        ag_ref[units, :] += tn(dts[k][...], part_ref[part])
    ffn_act(z, pre_ref[:u], pre_ref[u:], ag_ref[...], act_ref, gu_ref)
    for k in range(L):
        line_ref[lax.rem(at.l + k, L)] = nn(gus[k][...], gu_ref[...]).astype(bf16)
    for d in range(z.nd):
        out = jnp.concatenate([line_ref[z.fold * d + i] for i in range(z.fold)], axis=0)
        give_slots(z, out, d, mine_ref, other_ref)


def ffn_call(z, n2s, cots, gus, dts):
    t, L, u = z.tokens, z.length, z.units
    outs = [
        sds((4, z.nd, z.qw, t), bf16),
        sds((4, z.nd, z.qw, t), bf16),
        sds((2 * u, 8 * t), bf16),
        sds((u, 8 * t), bf16),
        sds((z.width, 8 * t), bf16),
        sds((z.width, 8 * t), bf16),
    ]
    flops = 2 * 8 * t * z.width * 5 * u
    if z.fold == 1:
        firsts = [
            sds((6 * z.rows, 3 * u), bf16),
            sds((2 * u, 6 * z.rows), bf16),
            outs[5],
            sds((u, 8 * t), f32),
        ]
        near = [gus[k] for k in KEPT[:3]]
        w, turned, cot, grad = call(ffn_first_kernel, z, firsts, cots + near, (), flops // 5)
        args = [w, turned, grad, cot, gus[KEPT[3]]] + n2s
        return list(call(ffn_kernel, z, outs[:5], args, (), flops)) + [cot]
    scratch = [
        pltpu.VMEM((2 * u, 8 * t), f32),
        pltpu.VMEM((u, 8 * t), f32),
        pltpu.VMEM((L, 2 * z.rows, 8 * t), bf16),
        pltpu.VMEM((z.nd, z.qw, 8 * t), bf16),
    ]
    return call(ffn_blocks_kernel, z, outs, n2s + cots + gus + dts, scratch, flops)


def down_part(z, l):
    i = lax.rem(l, z.fold)
    rows = slice(None) if z.fold == 1 else pl.ds(pl.multiple_of(i * z.down_rows, z.down_rows), z.down_rows)
    return l // z.fold, rows


def hidden_kernel(z, act_ref, *refs):
    L, u = z.length, z.units
    dts, (mine_ref, other_ref, sum_ref) = refs[:L], refs[L:]
    at = place()
    if z.fold == 1:
        for k in range(L):
            give_slots(z, nn(dts[k][:, 2 * u :], act_ref[...]), seen(z, at, k), mine_ref, other_ref)
    else:
        sum_ref[...] = jnp.zeros_like(sum_ref)
        for k in range(L):
            part, units = down_part(z, lax.rem(at.l + k, L))
            sum_ref[part] += nn(dts[k][...], act_ref[units, :])
        for d in range(z.nd):
            give_slots(z, sum_ref[d], d, mine_ref, other_ref)


def hidden_call(z, act, dts):
    t = z.tokens
    outs = [sds((4, z.nd, z.qw, t), bf16)] * 2
    scratch = [pltpu.VMEM((z.nd, z.qw, 8 * t) if z.fold != 1 else (8, 128), f32)]
    return call(hidden_kernel, z, outs, [act] + dts, scratch, 16 * t * z.width * z.units)


def ffn_weights_kernel(z, gu_ref, act_ref, n2_ref, cot_ref, *refs):
    L, u = z.length, z.units
    at = place()
    for n in range(L):
        k = KEPT[n] if z.fold == 1 else n
        rows = slice(2 * z.rows * n, 2 * z.rows * (n + 1))
        if z.fold == 1:
            refs[k][:, : 2 * u] = nt(n2_ref[rows, :], gu_ref[...]).astype(bf16)
            refs[k][:, 2 * u :] = nt(cot_ref[rows, :], act_ref[...]).astype(bf16)
        else:
            refs[2 * L][k] = nt(n2_ref[rows, :], gu_ref[...]).astype(bf16)
    if z.fold != 1:
        for d in range(z.nd):
            down = nt(cot_ref[z.qw * d : z.qw * (d + 1), :], act_ref[...])
            for i in range(z.fold):
                block = down[:, z.down_rows * i : z.down_rows * (i + 1)]
                refs[2 * L + 1][z.fold * d + i] = block.astype(bf16)
        for k in range(L):
            l = lax.rem(at.l + k, L)
            refs[k][...] = refs[2 * L][l]
            refs[L + k][...] = refs[2 * L + 1][l]


def ffn_weights_call(z, gu, act, n2, cot):
    L, scratch = z.length, []
    if z.fold == 1:
        outs = [sds((2 * z.rows, 3 * z.units), bf16)] * L
    else:
        shapes = (2 * z.rows, 2 * z.units), (z.qw, z.down_rows)
        outs = [sds(shape, bf16) for shape in shapes for _ in range(L)]
        scratch = [pltpu.VMEM((L,) + shape, bf16) for shape in shapes]
    flops = 2 * 8 * z.tokens * z.width * 3 * z.units
    out = call(ffn_weights_kernel, z, outs, [gu, act, n2, cot], scratch, flops)
    return out[:L], out[L:]


def core_sum(mine, got):
    total = [mine[i].astype(f32) + got[i].astype(f32) for i in range(4)]
    return [total[0]] + [part.astype(bf16) for part in total[1:]]


def slab_sum(z, own, got):
    out = []
    for k in range(z.length):
        n = own.shape[0] // z.length
        part = k if own.ndim == 3 else slice(n * k, n * (k + 1))
        total = own[part]
        for g in got:
            total = total + g[part].astype(f32)
        out.append(total if k == 0 else total.astype(bf16))
    return out


def backward_kernel(z, small_ref, places_ref, q_ref, mid_ref, inv_ref, gain_ref, cot_ref, mix_ref, lse_ref, cos_ref, sin_ref, own_ref, *refs):
    n = z.nc
    got, refs = refs[:3], refs[3:]
    chunks, pieces = refs[:n], refs[n : n + 8]
    midg_ref, midb_ref, gain_two_ref, dq_ref, *dkv_refs = refs[n + 8 : 2 * n + 12]
    kv_ref, bias_ref, grad_ref, dk_ref, rows_ref, dq_rows_ref = refs[2 * n + 12 :]
    at = place()
    t = z.tokens
    inv = inv_ref[0:1, :]
    mean = jnp.zeros((1, t), f32)
    for d in range(z.nd):
        g = own_ref[d] + got[0][d].astype(f32) + got[1][d].astype(f32) + got[2][d].astype(f32)
        mid = mid_ref[d]
        gain_two_ref[d] = jnp.broadcast_to(jnp.sum(g * mid * inv, axis=1, keepdims=True), (z.qw, 8))
        u = g * gain_ref[d][:, 1:2]
        midg_ref[d] = u
        mean = mean + jnp.sum(u * mid, axis=0, keepdims=True)
    scale = inv * inv * mean * (1.0 / z.width)
    for d in range(z.nd):
        full = cot_ref[d].astype(f32) + inv * (midg_ref[d] - mid_ref[d] * scale)
        midg_ref[d] = full
        midb_ref[d] = full.astype(bf16)
    part = slice(z.lane, z.lane + z.qw)
    for fy in (0, 1):
        acc = jnp.zeros((z.length * z.rows, t), f32)
        for piece, fx, fcore in pieces_of(pieces, fy):
            acc = acc + nn(piece[:, part], midb_ref[d_of(at, fx, fcore)])
        for k in range(z.length):
            grad_ref[c_of(z, at, fy, k)] = acc[z.rows * k : z.rows * (k + 1)]
    lay_keys(z, at, chunks, small_ref, places_ref, kv_ref, bias_ref)
    rows_ref[...] = jnp.concatenate([grad_ref[c] for c in range(z.nc)], axis=0)
    cos, sin = cos_ref[...], sin_ref[...]
    factor = HD**-0.5

    def head(h):
        q3 = three(q_ref, h)
        g3 = three(rows_ref, h).astype(bf16)
        delta = jnp.sum(g3.astype(f32) * three(mix_ref, h).astype(f32), axis=0, keepdims=True)
        key, value = head_of(kv_ref, h), head_of(kv_ref, KVH + h)
        p = jnp.exp(scores(kv_ref, bias_ref, h, q3) - lse_ref[pl.ds(h, 1), :])
        dv = nt(g3, p.astype(bf16))
        ds = (p * (tn(value, g3) - delta)).astype(bf16)
        dk = nt(q3, ds) * factor
        dq = nn(key, ds) * factor
        put_head(dk_ref, h, dk.astype(bf16))
        put_head(dk_ref, KVH + h, dv.astype(bf16))
        for g in range(GRP):
            put_head(dq_rows_ref, GRP * h + g, dq[:, t * g : t * (g + 1)])

    each_head(z, head)
    rows = rotate(dq_rows_ref[...], cos, -sin)
    for d in range(z.nd):
        dq_ref[d] = rows[z.qw * d : z.qw * (d + 1)].astype(bf16)
    for i, out in enumerate(dkv_refs):
        out[...] = dk_ref[:, t * i : t * (i + 1)]


def backward_call(z, small, places, q, mid, inv, gain_d, cot_d, mix, lse, cos, sin, own, got, chunks, pieces):
    t = z.tokens
    outs = [
        sds((z.nd, z.qw, t), f32),
        sds((z.nd, z.qw, t), bf16),
        sds((z.nd, z.qw, 8), f32),
        sds((z.nd, z.qw, t), bf16),
    ] + [sds((2 * KVW, t), bf16)] * z.nc
    scratch = [
        pltpu.VMEM((2 * KVW, z.nc * t), bf16),
        pltpu.VMEM((z.nc * t, t), f32),
        pltpu.VMEM((z.nc, z.rows, t), f32),
        pltpu.VMEM((2 * KVW, z.nc * t), bf16),
    ] + [pltpu.VMEM((QH * HD, t), f32)] * 2
    args = [small, places, q, mid, inv, gain_d, cot_d, mix, lse, cos, sin, own] + list(got) + chunks + pieces
    flops = 10 * z.nc * t * t * QH * HD + 2 * t * z.width**2
    return call(backward_kernel, z, outs, args, scratch, flops)


def qo_weights_kernel(z, n1_ref, mix_ref, dq_ref, midb_ref, gain_two_ref, *refs):
    pieces, (mine_ref, other_ref, nog_ref) = refs[:8], refs[8:]
    at = place()
    fill = jnp.zeros((z.length * z.rows, z.lane - z.qw - 8), f32)
    for fy in (0, 1):
        gain = jnp.concatenate([gathered(z, at, gain_two_ref, fy), fill], axis=1)
        acc = jnp.zeros((z.length * z.rows, z.tokens), f32)
        for piece, fx, fcore in pieces_of(pieces, fy)[::-1]:
            d, out = d_of(at, fx, fcore), other_ref if fcore else mine_ref
            block = jnp.concatenate([nt(n1_ref[fy], dq_ref[d]), gain], axis=1)
            out[fx + 2 * fy, :, : z.lane] = block.astype(bf16)
            out[fx + 2 * fy, :, z.lane :] = nt(mix_ref[fy], midb_ref[d]).astype(bf16)
            acc = acc + nn(piece[:, : z.qw], dq_ref[d])
        nog_ref[fy] = acc


def qo_weights_call(z, n1, mix, dq, midb, gain_two, pieces):
    blocks = (4, z.length * z.rows, z.lane + z.qw)
    outs = [sds(blocks, bf16), sds(blocks, bf16), sds(n1.shape, f32)]
    args = [n1, mix, dq, midb, gain_two] + pieces
    return call(qo_weights_kernel, z, outs, args, (), 6 * z.tokens * z.width**2)


def end_kernel(z, x_ref, inv_ref, gain_ref, n1_ref, midg_ref, nog_ref, cos_ref, sin_ref, own_ref, *refs):
    got, refs = refs[: z.length], refs[z.length :]
    pieces, (grad_ref, mine_ref, other_ref, dkv_ref, u_ref) = refs[:8], refs[8:]
    at = place()
    t, w = z.tokens, 2 * z.kw
    total = own_ref[...].astype(f32)
    for g in got:
        total = total + g[...].astype(f32)
    dk = rotate(total[:KVW], cos_ref[...], -sin_ref[...])
    for d in range(z.nd):
        dkv_ref[d, : z.kw] = dk[z.kw * d : z.kw * (d + 1)].astype(bf16)
        dkv_ref[d, z.kw :] = total[KVW + z.kw * d : KVW + z.kw * (d + 1)].astype(bf16)
    inv = inv_ref[0:1, :]
    mean = jnp.zeros((1, t), f32)
    columns = [(fx, fcore) for _, fx, fcore in pieces_of(pieces, 0)]
    every = jnp.concatenate([dkv_ref[d_of(at, fx, fcore)] for fx, fcore in columns], axis=0)
    for fy in (0, 1):
        nog = nog_ref[fy]
        for k in range(z.length):
            c = c_of(z, at, fy, k)
            block = slice(z.rows * k, z.rows * (k + 1))
            weights = jnp.concatenate([p[k, :w, :] for p, _, _ in pieces_of(pieces, fy)], axis=0)
            acc = nog[block] + tn(weights, every)
            x = x_ref[c].astype(f32)
            row = jnp.sum(jnp.transpose(acc * x * inv), axis=0, keepdims=True)
            gain = jnp.broadcast_to(row, (8, z.rows)).astype(bf16)
            u = acc * gain_ref[c][:, 0:1]
            u_ref[c] = u
            mean = mean + jnp.sum(u * x, axis=0, keepdims=True)
            terms = nt(every, n1_ref[fy][block]).astype(bf16)
            for i, (fx, fcore) in enumerate(columns):
                out = other_ref if fcore else mine_ref
                out[fx + 2 * fy, k, :w] = terms[w * i : w * (i + 1)]
                out[fx + 2 * fy, k, w : w + 8] = gain
    scale = inv * inv * mean * (1.0 / z.width)
    for c in range(z.nc):
        x = x_ref[c].astype(f32)
        grad_ref[c] = midg_ref[c] + inv * (u_ref[c] - x * scale)


def end_call(z, x_c, inv, gain, n1, midg_c, nog, cos, sin, own, got, pieces):
    t = z.tokens
    blocks = (4, z.length, 2 * z.kw + 8, z.rows)
    outs = [sds((z.nc, z.rows, t), f32), sds(blocks, bf16), sds(blocks, bf16)]
    scratch = [pltpu.VMEM((z.nd, 2 * z.kw, t), bf16), pltpu.VMEM((z.nc, z.rows, t), f32)]
    args = [x_c, inv, gain, n1, midg_c, nog, cos, sin, own] + got + pieces
    return call(end_kernel, z, outs, args, scratch, 8 * t * z.width * KVW)


def layer(
    nd, nc, hidden_in, positions, attn_gain, query_w, key_w, value_w, output_w,
    ffn_gain, gate_w, up_w, down_w, cotangent,
):
    _, tokens, width = hidden_in.shape
    z = SimpleNamespace(nd=nd, nc=nc, length=nc // 2, tokens=tokens, width=width, rows=width // nc)
    z.qw, z.kw, z.units = query_w.shape[1], key_w.shape[1], gate_w.shape[1] // 2
    z.down_rows, z.fold = down_w.shape[0], nc // (2 * nd)
    z.lane = -(-(z.qw + 8) // 128) * 128
    z.dt_lane = 2 * z.units if z.fold == 1 else 0
    L, t, rows = z.length, tokens, z.rows
    grad_scale = float(tokens * nd * nc) ** (-0.5)
    y0 = lax.rem(lax.axis_index("ctx"), 2)

    x_t, cot_t = hidden_in[0].T, cotangent[0].T
    x_c, x_d, cot_d = x_t.reshape(nc, rows, t), x_t.reshape(nd, z.qw, t), cot_t.reshape(nd, z.qw, t)

    def along_line(x):
        return [x] + [from_line(z, x, k) for k in range(1, L)]

    def over_slab(x, relay=False):
        mine = [x] + [to_slot(z, x, i) for i in (1, 2)]
        if relay:
            mine += [to_slot(z, mine[2], 1)]
        else:
            mine += [to_slot(z, x, 3)]
        return mine + [to_core(z, p) for p in mine]

    def flat(x):
        return x.reshape((L * x.shape[1],) + x.shape[2:])

    kv_line = along_line(first_call(z, key_w.T, value_w.T, attn_gain, ffn_gain, positions))
    kv_w = over_slab(jnp.stack(kv_line))

    pad = z.lane - z.qw
    qo = jnp.concatenate([jnp.pad(query_w, ((0, 0), (0, pad))), output_w], axis=1)
    qo_line = along_line(qo)
    qo_w = over_slab(flat(jnp.stack(qo_line)), relay=True)

    def own_half(w, other):
        low = (y0 == 0) != other
        return jnp.where(low, w[:, : z.units], w[:, z.units :])

    keep = jnp.concatenate([own_half(gate_w, False), own_half(up_w, False)], axis=1)
    give = jnp.concatenate([own_half(gate_w, True), own_half(up_w, True)], axis=1)
    take = to_slot(z, give, 2)
    gate_up = jnp.where(
        y0 == 0, jnp.concatenate([keep, take], axis=0), jnp.concatenate([take, keep], axis=0)
    )

    def down_target(d, c):
        n, i = c // z.fold, c % z.fold
        return n // 2, 2 * (z.fold * d + i) + n % 2

    down_back = {down_target(d, c): (d, c) for d in range(nd) for c in range(nc)}
    down_t = moved(z, down_w.T, down_target)
    if z.fold == 1:
        gus = line_pieces(z, jnp.concatenate([gate_up, down_t], axis=1))
        dts = gus
    else:
        gus, dts = line_pieces(z, gate_up), line_pieces(z, down_t)

    frequency = jnp.power(rope_base, -2.0 * jnp.arange(HALF, dtype=f32) / HD)
    angles = frequency[:, None] * positions[0].astype(f32)[None, :]
    cos, sin = jnp.cos(angles), jnp.sin(angles)
    kv, n1, inv_one, gain, small = kv_call(z, x_c, cos, sin, kv_w)
    gain_d = gain.reshape(nd, z.qw, 8)
    kv_along = along_line(kv)
    chunks = kv_along + [to_slot(z, p, 2) for p in kv_along]
    q = q_call(z, n1, cos, sin, qo_w)
    mix, mix_rows, lse, mid, inv_two, n2 = forward_call(z, small, positions, q, x_d, gain_d, chunks, qo_w)

    cots = over_slab(cot_d, relay=True)
    n2s = over_slab(n2.reshape(width, t))
    ntg_mine, ntg_other, gu, act, n2_all, cot_all = ffn_call(z, n2s, cots, gus, dts)
    ntg_own, *ntg_send = core_sum(ntg_mine, to_core(z, ntg_other))
    ntg_got = [to_slot(z, s, i + 1) for i, s in enumerate(ntg_send)]

    hid_mine, hid_other = hidden_call(z, act, dts)
    hid_own, *hid_send = core_sum(hid_mine, to_core(z, hid_other))
    gu_grads, dt_grads = ffn_weights_call(z, gu, act, n2_all, cot_all)

    midg, midb, gain_two, dq, *dkv = backward_call(
        z, small, positions, q, mid, inv_two, gain_d, cot_d, mix_rows, lse, cos, sin,
        ntg_own, ntg_got, chunks, qo_w,
    )

    dkv_got = []
    for k in range(L):
        got = to_slot(z, dkv[L + k], 2)
        if k == 0:
            dkv_got.append(got)
        else:
            both = (dkv[k].astype(f32) + got.astype(f32)).astype(bf16)
            dkv_got.append(from_line(z, both, -k))

    qo_mine, qo_other, nog = qo_weights_call(
        z, n1, mix, dq, midb, gain_two.reshape(nc, rows, 8), qo_w
    )
    grad_in, kv_mine, kv_other = end_call(
        z, x_c, inv_one, gain, n1, midg.reshape(nc, rows, t), nog, cos, sin, dkv[0], dkv_got, kv_w
    )

    def to_owner(mine, other):
        own, *sends = core_sum(mine, to_core(z, other))
        got = [to_slot(z, s, i + 1) for i, s in enumerate(sends)]
        return line_sum(slab_sum(z, own, got))

    def line_sum(pieces):
        total = pieces[0].astype(f32)
        for k in range(1, L):
            total = total + from_line(z, pieces[k], -k).astype(f32)
        return total * grad_scale

    def line_reduce(pieces):
        if L != 4:
            return line_sum(pieces)
        passed = from_line(z, pieces[2], 1)
        three = (pieces[3].astype(f32) + passed.astype(f32)).astype(bf16)
        total = pieces[0].astype(f32) + from_line(z, pieces[1], -1).astype(f32)
        return (total + from_line(z, three, -3).astype(f32)) * grad_scale

    sum_kv = to_owner(kv_mine, kv_other)
    sum_qo = to_owner(qo_mine, qo_other)

    hid_got = [to_slot(z, s, i + 1) for i, s in enumerate(hid_send)]
    hidden_out = mid + hid_own
    for g in hid_got:
        hidden_out = hidden_out + g.astype(f32)

    s_gu = line_reduce(gu_grads)
    s_dt = s_gu[:, 2 * z.units :] if z.fold == 1 else line_reduce(dt_grads)
    s_gu = s_gu[:, : 2 * z.units]
    mine = jnp.where(y0 == 0, s_gu[:rows], s_gu[rows:])
    theirs = jnp.where(y0 == 0, s_gu[rows:], s_gu[:rows]).astype(bf16)
    theirs = to_slot(z, theirs, 2).astype(f32)
    s_dt = moved(z, s_dt.astype(bf16), lambda d, c: down_back[(d, c)])
    low, high = jnp.where(y0 == 0, mine, theirs), jnp.where(y0 == 0, theirs, mine)
    grad_gate = jnp.concatenate([low[:, : z.units], high[:, : z.units]], axis=1)
    grad_up = jnp.concatenate([low[:, z.units :], high[:, z.units :]], axis=1)
    grad_down = s_dt.astype(f32).T

    kw, qw, w = z.kw, z.qw, 2 * z.kw
    return (
        hidden_out.reshape(width, t).T[None],
        grad_in.reshape(width, t).T[None],
        sum_kv[w],
        sum_qo[:, :qw],
        sum_kv[:kw].T,
        sum_kv[kw:w].T,
        sum_qo[:, z.lane :],
        sum_qo[:, qw],
        grad_gate,
        grad_up,
        grad_down,
    )


def solution(mesh):
    nd, nc = mesh.shape["dp"], mesh.shape["ctx"]
    whole, rows, gain = P("dp", "ctx", None), P("ctx", "dp"), P("ctx")
    in_specs = (whole, P("dp", "ctx"), gain, rows, rows, rows, rows, gain, rows, rows, rows, whole)
    out_specs = (whole, whole, gain, rows, rows, rows, rows, gain, rows, rows, rows)
    return jax.shard_map(
        functools.partial(layer, nd, nc),
        mesh=mesh,
        in_specs=in_specs,
        out_specs=out_specs,
        check_vma=False,
    )
```

```python
import functools
from types import SimpleNamespace

import jax
import jax.numpy as jnp
from jax import lax
from jax.experimental import pallas as pl
from jax.experimental.pallas import tpu as pltpu
from jax.sharding import PartitionSpec as P


QH = 15
KVH = 5
HD = 64
HALF = HD // 2
GRP = QH // KVH
KVW = KVH * HD
eps = 1e-05
rope_base = 10000.0
neg_big = -1e30
AX = ("dp", "ctx")
f32 = jnp.float32
bf16 = jnp.bfloat16


SLOTS = ((0, 0), (1, 0), (0, 1), (1, 1))


def moved(z, x, target):
    table = []
    for d in range(z.nd):
        for c in range(z.nc):
            dd, cc = target(d, c)
            table.append((d * z.nc + c, dd * z.nc + cc))
    return lax.ppermute(x, AX, table)


def to_slot(z, x, i):
    fx, fy = SLOTS[i]
    return moved(z, x, lambda d, c: (d ^ (2 * fx), c ^ fy))


def to_core(z, x):
    return moved(z, x, lambda d, c: (d ^ 1, c))


def from_line(z, x, k):
    k = k % z.length
    return moved(z, x, lambda d, c: (d, 2 * ((c // 2 - k) % z.length) + c % 2))


def line_pieces(z, x):
    if z.length != 4:
        return [x] + [from_line(z, x, k) for k in range(1, z.length)]
    one, three = from_line(z, x, 1), from_line(z, x, 3)
    return [x, one, from_line(z, one, 1), three]


def nt(a, b):
    return lax.dot_general(a, b, (((1,), (1,)), ((), ())), preferred_element_type=f32)


def nn(a, b):
    return lax.dot_general(a, b, (((1,), (0,)), ((), ())), preferred_element_type=f32)


def tn(a, b):
    return lax.dot_general(a, b, (((0,), (0,)), ((), ())), preferred_element_type=f32)


def place():
    d0, c0 = lax.axis_index("dp"), lax.axis_index("ctx")
    return SimpleNamespace(x=d0 // 2, core=lax.rem(d0, 2), l=c0 // 2, y=lax.rem(c0, 2))


def flip(bit, f):
    return 1 - bit if f else bit


def d_of(at, fx, fcore):
    return 2 * flip(at.x, fx) + flip(at.core, fcore)


def c_of(z, at, fy, k):
    return 2 * lax.rem(at.l + k, z.length) + flip(at.y, fy)


def pieces_of(pieces, fy):
    return [(pieces[4 * fcore + fx + 2 * fy], fx, fcore) for fcore in (0, 1) for fx in (0, 1)]


def gathered(z, at, ref, fy):
    return jnp.concatenate([ref[c_of(z, at, fy, k)] for k in range(z.length)], axis=0)


def seen(z, at, k):
    return lax.rem(at.l + k, z.nd) if z.fold == 1 else k


VM = pl.BlockSpec(memory_space=pltpu.VMEM)


def call(kernel, z, outs, args, scratch=(), flops=0):
    moved_bytes = sum(a.size * a.dtype.itemsize for a in args)
    moved_bytes += sum(o.size * o.dtype.itemsize for o in outs)
    return pl.pallas_call(
        functools.partial(kernel, z),
        out_shape=tuple(outs),
        in_specs=[VM] * len(args),
        out_specs=tuple([VM] * len(outs)),
        scratch_shapes=list(scratch),
        compiler_params=pltpu.CompilerParams(vmem_limit_bytes=56 << 20),
        cost_estimate=pl.CostEstimate(
            flops=int(flops), transcendentals=0, bytes_accessed=int(moved_bytes)
        ),
    )(*args)


def sds(shape, dtype):
    return jax.ShapeDtypeStruct(shape, dtype)


def rotate(rows, cos, sin):
    out = []
    for i in range(rows.shape[0] // HD):
        a, b = rows[HD * i : HD * i + HALF], rows[HD * i + HALF : HD * (i + 1)]
        out += [a * cos - b * sin, b * cos + a * sin]
    return jnp.concatenate(out, axis=0)


def first_kernel(z, key_ref, value_ref, gain_one_ref, gain_two_ref, places_ref, out_ref):
    half = z.tokens // 2
    blocks = [places_ref[0:1, half * i : half * i + 1].astype(f32) * (1.0 / half) for i in (0, 1)]
    rows = [gain_one_ref[...].astype(f32), gain_two_ref[...].astype(f32)]
    rows += [jnp.broadcast_to(b, (1, z.rows)) for b in blocks]
    rows += [jnp.zeros((4, z.rows), f32)]
    out_ref[: z.kw] = key_ref[...]
    out_ref[z.kw : 2 * z.kw] = value_ref[...]
    out_ref[2 * z.kw :] = jnp.concatenate(rows, axis=0).astype(bf16)


def first_call(z, key, value, gain_one, gain_two, places):
    outs = [sds((2 * z.kw + 8, z.rows), bf16)]
    args = [key, value, gain_one[None], gain_two[None], places]
    return call(first_kernel, z, outs, args)[0]


def kv_kernel(z, x_ref, cos_ref, sin_ref, *refs):
    pieces, (kv_ref, n1_ref, inv_ref, gain_ref, small_ref, acc_ref, sum_ref) = refs[:8], refs[8:]
    at = place()
    x = x_ref[...].astype(f32)
    mean = jnp.sum(jnp.sum(x * x, axis=0), axis=0, keepdims=True) * (1.0 / z.width)
    inv = lax.rsqrt(mean + eps)
    inv_ref[...] = jnp.broadcast_to(inv, inv_ref.shape)
    w = 2 * z.kw
    for fy, n in ((0, 0), (1, 2)):
        blocks = []
        for k in range(z.length):
            c = c_of(z, at, fy, k)
            small = pieces[n][k, w : w + 8, :].astype(f32)
            small_ref[c] = small
            gain = jnp.transpose(small)
            gain_ref[c] = gain
            block = x_ref[c].astype(f32) * inv * gain[:, 0:1]
            blocks.append(block)
            weights = jnp.concatenate([p[k, :w, :] for p, _, _ in pieces_of(pieces, fy)], axis=0)
            out = nn(weights, block.astype(bf16))
            if fy == 0 and k == 0:
                sum_ref[...] = out
            else:
                sum_ref[...] += out
        n1_ref[fy] = jnp.concatenate(blocks, axis=0).astype(bf16)
    for i, (_, fx, fcore) in enumerate(pieces_of(pieces, 0)):
        acc_ref[d_of(at, fx, fcore)] = sum_ref[w * i : w * (i + 1)]
    key = jnp.concatenate([acc_ref[d, : z.kw] for d in range(z.nd)], axis=0)
    value = jnp.concatenate([acc_ref[d, z.kw :] for d in range(z.nd)], axis=0)
    kv_ref[:KVW] = rotate(key, cos_ref[...], sin_ref[...]).astype(bf16)
    kv_ref[KVW:] = value.astype(bf16)


def kv_call(z, x_c, cos, sin, pieces):
    t = z.tokens
    outs = [
        sds((2 * KVW, t), bf16),
        sds((2, z.length * z.rows, t), bf16),
        sds((8, t), f32),
        sds((z.nc, z.rows, 8), f32),
        sds((z.nc, 8, z.rows), f32),
    ]
    scratch = [pltpu.VMEM((z.nd, 2 * z.kw, t), f32), pltpu.VMEM((z.nd * 2 * z.kw, t), f32)]
    return call(kv_kernel, z, outs, [x_c, cos, sin] + pieces, scratch, 2 * t * z.width * 2 * KVW)


def q_kernel(z, n1_ref, cos_ref, sin_ref, *refs):
    pieces, (q_ref, acc_ref) = refs[:8], refs[8:]
    at = place()
    for (low, fx, fcore), (high, _, _) in zip(pieces_of(pieces, 0), pieces_of(pieces, 1)):
        out = tn(low[:, : z.qw], n1_ref[0]) + tn(high[:, : z.qw], n1_ref[1])
        acc_ref[d_of(at, fx, fcore)] = out
    q = jnp.concatenate([acc_ref[d] for d in range(z.nd)], axis=0)
    q_ref[...] = rotate(q, cos_ref[...], sin_ref[...]).astype(bf16)


def q_call(z, n1, cos, sin, pieces):
    scratch = [pltpu.VMEM((z.nd, z.qw, z.tokens), f32)]
    outs = [sds((QH * HD, z.tokens), bf16)]
    return call(q_kernel, z, outs, [n1, cos, sin] + pieces, scratch, 2 * z.tokens * z.width**2)[0]


def lay_keys(z, at, chunks, small_ref, places_ref, kv_ref, bias_ref):
    t = z.tokens
    row = lax.broadcasted_iota(jnp.int32, (t, t), 0)
    low = row < t // 2
    within = jnp.where(low, row, row - t // 2).astype(f32)
    places = places_ref[0:1, :].astype(f32)
    for n, chunk in enumerate(chunks):
        kv_ref[:, t * n : t * (n + 1)] = chunk[...]
        c = c_of(z, at, n // z.length, n % z.length)
        small = small_ref[c]
        start = jnp.where(low, small[2:3, 0:1], small[3:4, 0:1]) * float(t // 2)
        bias_ref[t * n : t * (n + 1), :] = jnp.where(start + within <= places, 0.0, neg_big)


def three(ref, h):
    return jnp.concatenate([head_of(ref, GRP * h + g) for g in range(GRP)], axis=1)


def scaled(q3):
    return (q3.astype(f32) * (HD**-0.5)).astype(bf16)


def scores(kv_ref, bias_ref, h, q3):
    s = tn(head_of(kv_ref, h), q3)
    bias = bias_ref[...]
    return s + jnp.concatenate([bias] * GRP, axis=1)


def each_head(z, body):
    if z.nc <= 8:
        for h in range(KVH):
            body(h)
    else:
        lax.fori_loop(0, KVH, lambda h, carry: (body(h), carry)[1], 0)


def head_of(ref, n):
    start = HD * n
    return ref[pl.ds(start if isinstance(n, int) else pl.multiple_of(start, HD), HD), :]


def put_head(ref, n, x):
    start = HD * n
    ref[pl.ds(start if isinstance(n, int) else pl.multiple_of(start, HD), HD), :] = x


def forward_kernel(z, small_ref, places_ref, q_ref, x_ref, gain_ref, *refs):
    n = z.nc
    chunks, pieces = refs[:n], refs[n : n + 8]
    mix_ref, rows_out_ref, lse_ref, mid_ref, inv_ref, n2_ref = refs[n + 8 : n + 14]
    kv_ref, bias_ref, rows_ref, block_ref = refs[n + 14 :]
    at = place()
    t = z.tokens
    lay_keys(z, at, chunks, small_ref, places_ref, kv_ref, bias_ref)

    def head(h):
        s = scores(kv_ref, bias_ref, h, scaled(three(q_ref, h)))
        top = jnp.max(s, axis=0, keepdims=True)
        e = jnp.exp(s - top)
        total = jnp.sum(e, axis=0, keepdims=True)
        lse_ref[pl.ds(h, 1), :] = top + jnp.log(total)
        p = (e * (1.0 / total)).astype(bf16)
        out = nn(head_of(kv_ref, KVH + h), p)
        for g in range(GRP):
            put_head(rows_ref, GRP * h + g, out[:, t * g : t * (g + 1)])

    each_head(z, head)
    mix = rows_ref[...]
    rows_out_ref[...] = mix.astype(bf16)
    for c in range(z.nc):
        block_ref[c] = mix[z.rows * c : z.rows * (c + 1)]
    for fy in (0, 1):
        mix_ref[fy] = gathered(z, at, block_ref, fy).astype(bf16)
    square = jnp.zeros((1, t), f32)
    part = slice(z.lane, z.lane + z.qw)
    for (low, fx, fcore), (high, _, _) in zip(pieces_of(pieces, 0), pieces_of(pieces, 1)):
        d = d_of(at, fx, fcore)
        mid = x_ref[d].astype(f32) + tn(low[:, part], mix_ref[0]) + tn(high[:, part], mix_ref[1])
        mid_ref[d] = mid
        square = square + jnp.sum(mid * mid, axis=0, keepdims=True)
    inv = lax.rsqrt(square * (1.0 / z.width) + eps)
    inv_ref[...] = jnp.broadcast_to(inv, inv_ref.shape)
    for k in range(z.nd):
        d = seen(z, at, k)
        n2_ref[k] = (mid_ref[d] * inv * gain_ref[d][:, 1:2]).astype(bf16)


def forward_call(z, small, places, q, x_d, gain_d, chunks, pieces):
    t = z.tokens
    outs = [
        sds((2, z.length * z.rows, t), bf16),
        sds((QH * HD, t), bf16),
        sds((8, GRP * t), f32),
        sds((z.nd, z.qw, t), f32),
        sds((8, t), f32),
        sds((z.nd, z.qw, t), bf16),
    ]
    scratch = [
        pltpu.VMEM((2 * KVW, z.nc * t), bf16),
        pltpu.VMEM((z.nc * t, t), f32),
        pltpu.VMEM((QH * HD, t), f32),
        pltpu.VMEM((z.nc, z.rows, t), f32),
    ]
    args = [small, places, q, x_d, gain_d] + chunks + pieces
    flops = 4 * z.nc * t * t * QH * HD + 2 * t * z.width**2
    return call(forward_kernel, z, outs, args, scratch, flops)


def ffn_act(z, gate, up, act_grad, act_ref, gu_ref):
    u = z.units
    sigma = jax.nn.sigmoid(gate)
    gs = gate * sigma
    act_ref[...] = (gs * up).astype(bf16)
    gu_ref[:u] = (act_grad * up * sigma * (1.0 + gate * (1.0 - sigma))).astype(bf16)
    gu_ref[u:] = (act_grad * gs).astype(bf16)


def give_slots(z, out, d, mine_ref, other_ref):
    t = z.tokens
    for i in range(4):
        mine_ref[i, d] = out[:, t * i : t * (i + 1)].astype(bf16)
        other_ref[i, d] = out[:, t * (4 + i) : t * (5 + i)].astype(bf16)


KEPT = (0, 1, 3, 2)


def ffn_first_kernel(z, *refs):
    t, u, b = z.tokens, z.units, 2 * z.rows
    cots, ws = refs[:8], refs[8:11]
    w_ref, turned_ref, cot_ref, grad_ref = refs[11:]
    at = place()
    for n, k in enumerate(KEPT):
        if n < 3:
            w_ref[b * n : b * (n + 1), :] = ws[n][...]
        for i in range(8):
            cot_ref[b * n : b * (n + 1), t * i : t * (i + 1)] = cots[i][seen(z, at, k)]
    turned_ref[...] = jnp.transpose(w_ref[:, : 2 * u])
    grad_ref[...] = tn(w_ref[:, 2 * u :], cot_ref[: 3 * b, :])


def ffn_kernel(z, w_ref, turned_ref, grad_ref, cot_ref, far_ref, *refs):
    n2s, (mine_ref, other_ref, gu_ref, act_ref, n2_ref) = refs[:8], refs[8:]
    t, u, b = z.tokens, z.units, 2 * z.rows
    at = place()
    for n, k in enumerate(KEPT):
        for i in range(8):
            n2_ref[b * n : b * (n + 1), t * i : t * (i + 1)] = n2s[i][b * k : b * (k + 1), :]
    gate_up = nn(turned_ref[...], n2_ref[: 3 * b, :]) + tn(far_ref[:, : 2 * u], n2_ref[3 * b :, :])
    act_grad = grad_ref[...] + tn(far_ref[:, 2 * u :], cot_ref[3 * b :, :])
    ffn_act(z, gate_up[:u], gate_up[u:], act_grad, act_ref, gu_ref)
    for n, k in enumerate(KEPT):
        w = far_ref[:, : 2 * u] if n == 3 else w_ref[b * n : b * (n + 1), : 2 * u]
        give_slots(z, nn(w, gu_ref[...]), seen(z, at, k), mine_ref, other_ref)


def ffn_blocks_kernel(z, *refs):
    L = z.length
    n2s, cots, gus, dts = refs[:8], refs[8:16], refs[16 : 16 + L], refs[16 + L : 16 + 2 * L]
    mine_ref, other_ref, gu_ref, act_ref, n2_ref, cot_ref, pre_ref, ag_ref, line_ref, part_ref = refs[16 + 2 * L :]
    at = place()
    u, rows = z.units, 2 * z.rows
    t = z.tokens
    for i in range(8):
        n2_ref[:, t * i : t * (i + 1)] = n2s[i][...]
        for d in range(z.nd):
            part_ref[d, :, t * i : t * (i + 1)] = cots[i][d]
            cot_ref[z.qw * d : z.qw * (d + 1), t * i : t * (i + 1)] = cots[i][d]
    for l in range(L):
        line_ref[l] = n2_ref[rows * l : rows * (l + 1), :]
    pre_ref[...] = jnp.zeros_like(pre_ref)
    ag_ref[...] = jnp.zeros_like(ag_ref)
    for k in range(L):
        l = lax.rem(at.l + k, L)
        part, units = down_part(z, l)
        pre_ref[...] += tn(gus[k][...], line_ref[l])
        ag_ref[units, :] += tn(dts[k][...], part_ref[part])
    ffn_act(z, pre_ref[:u], pre_ref[u:], ag_ref[...], act_ref, gu_ref)
    for k in range(L):
        line_ref[lax.rem(at.l + k, L)] = nn(gus[k][...], gu_ref[...]).astype(bf16)
    for d in range(z.nd):
        out = jnp.concatenate([line_ref[z.fold * d + i] for i in range(z.fold)], axis=0)
        give_slots(z, out, d, mine_ref, other_ref)


def ffn_call(z, n2s, cots, gus, dts):
    t, L, u = z.tokens, z.length, z.units
    outs = [
        sds((4, z.nd, z.qw, t), bf16),
        sds((4, z.nd, z.qw, t), bf16),
        sds((2 * u, 8 * t), bf16),
        sds((u, 8 * t), bf16),
        sds((z.width, 8 * t), bf16),
        sds((z.width, 8 * t), bf16),
    ]
    flops = 2 * 8 * t * z.width * 5 * u
    if z.fold == 1:
        firsts = [
            sds((6 * z.rows, 3 * u), bf16),
            sds((2 * u, 6 * z.rows), bf16),
            outs[5],
            sds((u, 8 * t), f32),
        ]
        near = [gus[k] for k in KEPT[:3]]
        w, turned, cot, grad = call(ffn_first_kernel, z, firsts, cots + near, (), flops // 5)
        args = [w, turned, grad, cot, gus[KEPT[3]]] + n2s
        return list(call(ffn_kernel, z, outs[:5], args, (), flops)) + [cot]
    scratch = [
        pltpu.VMEM((2 * u, 8 * t), f32),
        pltpu.VMEM((u, 8 * t), f32),
        pltpu.VMEM((L, 2 * z.rows, 8 * t), bf16),
        pltpu.VMEM((z.nd, z.qw, 8 * t), bf16),
    ]
    return call(ffn_blocks_kernel, z, outs, n2s + cots + gus + dts, scratch, flops)


def down_part(z, l):
    i = lax.rem(l, z.fold)
    rows = slice(None) if z.fold == 1 else pl.ds(pl.multiple_of(i * z.down_rows, z.down_rows), z.down_rows)
    return l // z.fold, rows


def hidden_kernel(z, act_ref, *refs):
    L, u = z.length, z.units
    dts, (mine_ref, other_ref, sum_ref) = refs[:L], refs[L:]
    at = place()
    if z.fold == 1:
        for k in range(L):
            give_slots(z, nn(dts[k][:, 2 * u :], act_ref[...]), seen(z, at, k), mine_ref, other_ref)
    else:
        sum_ref[...] = jnp.zeros_like(sum_ref)
        for k in range(L):
            part, units = down_part(z, lax.rem(at.l + k, L))
            sum_ref[part] += nn(dts[k][...], act_ref[units, :])
        for d in range(z.nd):
            give_slots(z, sum_ref[d], d, mine_ref, other_ref)


def hidden_call(z, act, dts):
    t = z.tokens
    outs = [sds((4, z.nd, z.qw, t), bf16)] * 2
    scratch = [pltpu.VMEM((z.nd, z.qw, 8 * t) if z.fold != 1 else (8, 128), f32)]
    return call(hidden_kernel, z, outs, [act] + dts, scratch, 16 * t * z.width * z.units)


def ffn_weights_kernel(z, gu_ref, act_ref, n2_ref, cot_ref, *refs):
    L, u = z.length, z.units
    at = place()
    for n in range(L):
        k = KEPT[n] if z.fold == 1 else n
        rows = slice(2 * z.rows * n, 2 * z.rows * (n + 1))
        if z.fold == 1:
            refs[k][:, : 2 * u] = nt(n2_ref[rows, :], gu_ref[...]).astype(bf16)
            refs[k][:, 2 * u :] = nt(cot_ref[rows, :], act_ref[...]).astype(bf16)
        else:
            refs[2 * L][k] = nt(n2_ref[rows, :], gu_ref[...]).astype(bf16)
    if z.fold != 1:
        for d in range(z.nd):
            down = nt(cot_ref[z.qw * d : z.qw * (d + 1), :], act_ref[...])
            for i in range(z.fold):
                block = down[:, z.down_rows * i : z.down_rows * (i + 1)]
                refs[2 * L + 1][z.fold * d + i] = block.astype(bf16)
        for k in range(L):
            l = lax.rem(at.l + k, L)
            refs[k][...] = refs[2 * L][l]
            refs[L + k][...] = refs[2 * L + 1][l]


def ffn_weights_call(z, gu, act, n2, cot):
    L, scratch = z.length, []
    if z.fold == 1:
        outs = [sds((2 * z.rows, 3 * z.units), bf16)] * L
    else:
        shapes = (2 * z.rows, 2 * z.units), (z.qw, z.down_rows)
        outs = [sds(shape, bf16) for shape in shapes for _ in range(L)]
        scratch = [pltpu.VMEM((L,) + shape, bf16) for shape in shapes]
    flops = 2 * 8 * z.tokens * z.width * 3 * z.units
    out = call(ffn_weights_kernel, z, outs, [gu, act, n2, cot], scratch, flops)
    return out[:L], out[L:]


def core_sum(mine, got):
    total = [mine[i].astype(f32) + got[i].astype(f32) for i in range(4)]
    return [total[0]] + [part.astype(bf16) for part in total[1:]]


def slab_sum(z, own, got):
    out = []
    for k in range(z.length):
        n = own.shape[0] // z.length
        part = k if own.ndim == 3 else slice(n * k, n * (k + 1))
        total = own[part]
        for g in got:
            total = total + g[part].astype(f32)
        out.append(total if k == 0 else total.astype(bf16))
    return out


def backward_kernel(z, small_ref, places_ref, q_ref, mid_ref, inv_ref, gain_ref, cot_ref, mix_ref, lse_ref, cos_ref, sin_ref, own_ref, *refs):
    n = z.nc
    got, refs = refs[:3], refs[3:]
    chunks, pieces = refs[:n], refs[n : n + 8]
    midg_ref, midb_ref, gain_two_ref, dq_ref, *dkv_refs = refs[n + 8 : 2 * n + 12]
    kv_ref, bias_ref, grad_ref, dk_ref, rows_ref, dq_rows_ref = refs[2 * n + 12 :]
    at = place()
    t = z.tokens
    inv = inv_ref[0:1, :]
    mean = jnp.zeros((1, t), f32)
    for d in range(z.nd):
        g = own_ref[d] + got[0][d].astype(f32) + got[1][d].astype(f32) + got[2][d].astype(f32)
        mid = mid_ref[d]
        gain_two_ref[d] = jnp.broadcast_to(jnp.sum(g * mid * inv, axis=1, keepdims=True), (z.qw, 8))
        u = g * gain_ref[d][:, 1:2]
        midg_ref[d] = u
        mean = mean + jnp.sum(u * mid, axis=0, keepdims=True)
    scale = inv * inv * mean * (1.0 / z.width)
    for d in range(z.nd):
        full = cot_ref[d].astype(f32) + inv * (midg_ref[d] - mid_ref[d] * scale)
        midg_ref[d] = full
        midb_ref[d] = full.astype(bf16)
    part = slice(z.lane, z.lane + z.qw)
    for fy in (0, 1):
        acc = jnp.zeros((z.length * z.rows, t), f32)
        for piece, fx, fcore in pieces_of(pieces, fy):
            acc = acc + nn(piece[:, part], midb_ref[d_of(at, fx, fcore)])
        for k in range(z.length):
            grad_ref[c_of(z, at, fy, k)] = acc[z.rows * k : z.rows * (k + 1)]
    lay_keys(z, at, chunks, small_ref, places_ref, kv_ref, bias_ref)
    rows_ref[...] = jnp.concatenate([grad_ref[c] for c in range(z.nc)], axis=0)
    cos, sin = cos_ref[...], sin_ref[...]
    factor = HD**-0.5

    def head(h):
        q3 = scaled(three(q_ref, h))
        g3 = three(rows_ref, h).astype(bf16)
        delta = jnp.sum(g3.astype(f32) * three(mix_ref, h).astype(f32), axis=0, keepdims=True)
        key, value = head_of(kv_ref, h), head_of(kv_ref, KVH + h)
        p = jnp.exp(scores(kv_ref, bias_ref, h, q3) - lse_ref[pl.ds(h, 1), :])
        dv = nt(g3, p.astype(bf16))
        ds = (p * (tn(value, g3) - delta)).astype(bf16)
        dk = nt(q3, ds)
        dq = nn(key, ds) * factor
        put_head(dk_ref, h, dk.astype(bf16))
        put_head(dk_ref, KVH + h, dv.astype(bf16))
        for g in range(GRP):
            put_head(dq_rows_ref, GRP * h + g, dq[:, t * g : t * (g + 1)])

    each_head(z, head)
    rows = rotate(dq_rows_ref[...], cos, -sin)
    for d in range(z.nd):
        dq_ref[d] = rows[z.qw * d : z.qw * (d + 1)].astype(bf16)
    for i, out in enumerate(dkv_refs):
        out[...] = dk_ref[:, t * i : t * (i + 1)]


def backward_call(z, small, places, q, mid, inv, gain_d, cot_d, mix, lse, cos, sin, own, got, chunks, pieces):
    t = z.tokens
    outs = [
        sds((z.nd, z.qw, t), f32),
        sds((z.nd, z.qw, t), bf16),
        sds((z.nd, z.qw, 8), f32),
        sds((z.nd, z.qw, t), bf16),
    ] + [sds((2 * KVW, t), bf16)] * z.nc
    scratch = [
        pltpu.VMEM((2 * KVW, z.nc * t), bf16),
        pltpu.VMEM((z.nc * t, t), f32),
        pltpu.VMEM((z.nc, z.rows, t), f32),
        pltpu.VMEM((2 * KVW, z.nc * t), bf16),
    ] + [pltpu.VMEM((QH * HD, t), f32)] * 2
    args = [small, places, q, mid, inv, gain_d, cot_d, mix, lse, cos, sin, own] + list(got) + chunks + pieces
    flops = 10 * z.nc * t * t * QH * HD + 2 * t * z.width**2
    return call(backward_kernel, z, outs, args, scratch, flops)


def qo_weights_kernel(z, n1_ref, mix_ref, dq_ref, midb_ref, gain_two_ref, *refs):
    pieces, (mine_ref, other_ref, nog_ref) = refs[:8], refs[8:]
    at = place()
    fill = jnp.zeros((z.length * z.rows, z.lane - z.qw - 8), f32)
    for fy in (0, 1):
        gain = jnp.concatenate([gathered(z, at, gain_two_ref, fy), fill], axis=1)
        acc = jnp.zeros((z.length * z.rows, z.tokens), f32)
        for piece, fx, fcore in pieces_of(pieces, fy)[::-1]:
            d, out = d_of(at, fx, fcore), other_ref if fcore else mine_ref
            block = jnp.concatenate([nt(n1_ref[fy], dq_ref[d]), gain], axis=1)
            out[fx + 2 * fy, :, : z.lane] = block.astype(bf16)
            out[fx + 2 * fy, :, z.lane :] = nt(mix_ref[fy], midb_ref[d]).astype(bf16)
            acc = acc + nn(piece[:, : z.qw], dq_ref[d])
        nog_ref[fy] = acc


def qo_weights_call(z, n1, mix, dq, midb, gain_two, pieces):
    blocks = (4, z.length * z.rows, z.lane + z.qw)
    outs = [sds(blocks, bf16), sds(blocks, bf16), sds(n1.shape, f32)]
    args = [n1, mix, dq, midb, gain_two] + pieces
    return call(qo_weights_kernel, z, outs, args, (), 6 * z.tokens * z.width**2)


def end_kernel(z, x_ref, inv_ref, gain_ref, n1_ref, midg_ref, nog_ref, cos_ref, sin_ref, own_ref, *refs):
    got, refs = refs[: z.length], refs[z.length :]
    pieces, (grad_ref, mine_ref, other_ref, dkv_ref, u_ref) = refs[:8], refs[8:]
    at = place()
    t, w = z.tokens, 2 * z.kw
    total = own_ref[...].astype(f32)
    for g in got:
        total = total + g[...].astype(f32)
    dk = rotate(total[:KVW], cos_ref[...], -sin_ref[...])
    for d in range(z.nd):
        dkv_ref[d, : z.kw] = dk[z.kw * d : z.kw * (d + 1)].astype(bf16)
        dkv_ref[d, z.kw :] = total[KVW + z.kw * d : KVW + z.kw * (d + 1)].astype(bf16)
    inv = inv_ref[0:1, :]
    mean = jnp.zeros((1, t), f32)
    columns = [(fx, fcore) for _, fx, fcore in pieces_of(pieces, 0)]
    every = jnp.concatenate([dkv_ref[d_of(at, fx, fcore)] for fx, fcore in columns], axis=0)
    for fy in (0, 1):
        nog = nog_ref[fy]
        for k in range(z.length):
            c = c_of(z, at, fy, k)
            block = slice(z.rows * k, z.rows * (k + 1))
            weights = jnp.concatenate([p[k, :w, :] for p, _, _ in pieces_of(pieces, fy)], axis=0)
            acc = nog[block] + tn(weights, every)
            x = x_ref[c].astype(f32)
            row = jnp.sum(jnp.transpose(acc * x * inv), axis=0, keepdims=True)
            gain = jnp.broadcast_to(row, (8, z.rows)).astype(bf16)
            u = acc * gain_ref[c][:, 0:1]
            u_ref[c] = u
            mean = mean + jnp.sum(u * x, axis=0, keepdims=True)
            terms = nt(every, n1_ref[fy][block]).astype(bf16)
            for i, (fx, fcore) in enumerate(columns):
                out = other_ref if fcore else mine_ref
                out[fx + 2 * fy, k, :w] = terms[w * i : w * (i + 1)]
                out[fx + 2 * fy, k, w : w + 8] = gain
    scale = inv * inv * mean * (1.0 / z.width)
    for c in range(z.nc):
        x = x_ref[c].astype(f32)
        grad_ref[c] = midg_ref[c] + inv * (u_ref[c] - x * scale)


def end_call(z, x_c, inv, gain, n1, midg_c, nog, cos, sin, own, got, pieces):
    t = z.tokens
    blocks = (4, z.length, 2 * z.kw + 8, z.rows)
    outs = [sds((z.nc, z.rows, t), f32), sds(blocks, bf16), sds(blocks, bf16)]
    scratch = [pltpu.VMEM((z.nd, 2 * z.kw, t), bf16), pltpu.VMEM((z.nc, z.rows, t), f32)]
    args = [x_c, inv, gain, n1, midg_c, nog, cos, sin, own] + got + pieces
    return call(end_kernel, z, outs, args, scratch, 8 * t * z.width * KVW)


def layer(
    nd, nc, hidden_in, positions, attn_gain, query_w, key_w, value_w, output_w,
    ffn_gain, gate_w, up_w, down_w, cotangent,
):
    _, tokens, width = hidden_in.shape
    z = SimpleNamespace(nd=nd, nc=nc, length=nc // 2, tokens=tokens, width=width, rows=width // nc)
    z.qw, z.kw, z.units = query_w.shape[1], key_w.shape[1], gate_w.shape[1] // 2
    z.down_rows, z.fold = down_w.shape[0], nc // (2 * nd)
    z.lane = -(-(z.qw + 8) // 128) * 128
    z.dt_lane = 2 * z.units if z.fold == 1 else 0
    L, t, rows = z.length, tokens, z.rows
    grad_scale = float(tokens * nd * nc) ** (-0.5)
    y0 = lax.rem(lax.axis_index("ctx"), 2)

    x_t, cot_t = hidden_in[0].T, cotangent[0].T
    x_c, x_d, cot_d = x_t.reshape(nc, rows, t), x_t.reshape(nd, z.qw, t), cot_t.reshape(nd, z.qw, t)

    def along_line(x):
        return [x] + [from_line(z, x, k) for k in range(1, L)]

    def over_slab(x, relay=False):
        mine = [x] + [to_slot(z, x, i) for i in (1, 2)]
        if relay:
            mine += [to_slot(z, mine[2], 1)]
        else:
            mine += [to_slot(z, x, 3)]
        return mine + [to_core(z, p) for p in mine]

    def flat(x):
        return x.reshape((L * x.shape[1],) + x.shape[2:])

    kv_line = along_line(first_call(z, key_w.T, value_w.T, attn_gain, ffn_gain, positions))
    kv_w = over_slab(jnp.stack(kv_line))

    pad = z.lane - z.qw
    qo = jnp.concatenate([jnp.pad(query_w, ((0, 0), (0, pad))), output_w], axis=1)
    qo_line = along_line(qo)
    qo_w = over_slab(flat(jnp.stack(qo_line)), relay=True)

    def own_half(w, other):
        low = (y0 == 0) != other
        return jnp.where(low, w[:, : z.units], w[:, z.units :])

    keep = jnp.concatenate([own_half(gate_w, False), own_half(up_w, False)], axis=1)
    give = jnp.concatenate([own_half(gate_w, True), own_half(up_w, True)], axis=1)
    take = to_slot(z, give, 2)
    gate_up = jnp.where(
        y0 == 0, jnp.concatenate([keep, take], axis=0), jnp.concatenate([take, keep], axis=0)
    )

    def down_target(d, c):
        n, i = c // z.fold, c % z.fold
        return n // 2, 2 * (z.fold * d + i) + n % 2

    down_back = {down_target(d, c): (d, c) for d in range(nd) for c in range(nc)}
    down_t = moved(z, down_w.T, down_target)
    if z.fold == 1:
        gus = line_pieces(z, jnp.concatenate([gate_up, down_t], axis=1))
        dts = gus
    else:
        gus, dts = line_pieces(z, gate_up), line_pieces(z, down_t)

    frequency = jnp.power(rope_base, -2.0 * jnp.arange(HALF, dtype=f32) / HD)
    angles = frequency[:, None] * positions[0].astype(f32)[None, :]
    cos, sin = jnp.cos(angles), jnp.sin(angles)
    kv, n1, inv_one, gain, small = kv_call(z, x_c, cos, sin, kv_w)
    gain_d = gain.reshape(nd, z.qw, 8)
    kv_along = along_line(kv)
    chunks = kv_along + [to_slot(z, p, 2) for p in kv_along]
    q = q_call(z, n1, cos, sin, qo_w)
    mix, mix_rows, lse, mid, inv_two, n2 = forward_call(z, small, positions, q, x_d, gain_d, chunks, qo_w)

    cots = over_slab(cot_d, relay=True)
    n2s = over_slab(n2.reshape(width, t))
    ntg_mine, ntg_other, gu, act, n2_all, cot_all = ffn_call(z, n2s, cots, gus, dts)
    ntg_own, *ntg_send = core_sum(ntg_mine, to_core(z, ntg_other))
    ntg_got = [to_slot(z, s, i + 1) for i, s in enumerate(ntg_send)]

    hid_mine, hid_other = hidden_call(z, act, dts)
    hid_own, *hid_send = core_sum(hid_mine, to_core(z, hid_other))
    gu_grads, dt_grads = ffn_weights_call(z, gu, act, n2_all, cot_all)

    midg, midb, gain_two, dq, *dkv = backward_call(
        z, small, positions, q, mid, inv_two, gain_d, cot_d, mix_rows, lse, cos, sin,
        ntg_own, ntg_got, chunks, qo_w,
    )

    dkv_got = []
    for k in range(L):
        got = to_slot(z, dkv[L + k], 2)
        if k == 0:
            dkv_got.append(got)
        else:
            both = (dkv[k].astype(f32) + got.astype(f32)).astype(bf16)
            dkv_got.append(from_line(z, both, -k))

    qo_mine, qo_other, nog = qo_weights_call(
        z, n1, mix, dq, midb, gain_two.reshape(nc, rows, 8), qo_w
    )
    grad_in, kv_mine, kv_other = end_call(
        z, x_c, inv_one, gain, n1, midg.reshape(nc, rows, t), nog, cos, sin, dkv[0], dkv_got, kv_w
    )

    def to_owner(mine, other):
        own, *sends = core_sum(mine, to_core(z, other))
        got = [to_slot(z, s, i + 1) for i, s in enumerate(sends)]
        return line_sum(slab_sum(z, own, got))

    def line_sum(pieces):
        got = [from_line(z, pieces[k], -k) for k in range(1, L)]
        total = pieces[0].astype(f32)
        for g in got:
            total = total + g.astype(f32)
        return total * grad_scale

    def line_reduce(pieces):
        if L != 4:
            return line_sum(pieces)
        passed = from_line(z, pieces[2], 1)
        three = (pieces[3].astype(f32) + passed.astype(f32)).astype(bf16)
        total = pieces[0].astype(f32) + from_line(z, pieces[1], -1).astype(f32)
        return (total + from_line(z, three, -3).astype(f32)) * grad_scale

    sum_kv = to_owner(kv_mine, kv_other)
    sum_qo = to_owner(qo_mine, qo_other)
    grad_query, grad_out, grad_ffn_gain = sum_qo[:, : z.qw], sum_qo[:, z.lane :], sum_qo[:, z.qw]

    hid_got = [to_slot(z, s, i + 1) for i, s in enumerate(hid_send)]
    hidden_out = mid + hid_own
    for g in hid_got:
        hidden_out = hidden_out + g.astype(f32)

    s_gu = line_reduce(gu_grads)
    s_dt = s_gu[:, 2 * z.units :] if z.fold == 1 else line_reduce(dt_grads)
    s_gu = s_gu[:, : 2 * z.units]
    mine = jnp.where(y0 == 0, s_gu[:rows], s_gu[rows:])
    theirs = jnp.where(y0 == 0, s_gu[rows:], s_gu[:rows]).astype(bf16)
    theirs = to_slot(z, theirs, 2).astype(f32)
    s_dt = moved(z, s_dt.astype(bf16), lambda d, c: down_back[(d, c)])
    low, high = jnp.where(y0 == 0, mine, theirs), jnp.where(y0 == 0, theirs, mine)
    grad_gate = jnp.concatenate([low[:, : z.units], high[:, : z.units]], axis=1)
    grad_up = jnp.concatenate([low[:, z.units :], high[:, z.units :]], axis=1)
    grad_down = s_dt.astype(f32).T

    kw, w = z.kw, 2 * z.kw
    return (
        hidden_out.reshape(width, t).T[None],
        grad_in.reshape(width, t).T[None],
        sum_kv[w],
        grad_query,
        sum_kv[:kw].T,
        sum_kv[kw:w].T,
        grad_out,
        grad_ffn_gain,
        grad_gate,
        grad_up,
        grad_down,
    )


def solution(mesh):
    nd, nc = mesh.shape["dp"], mesh.shape["ctx"]
    whole, rows, gain = P("dp", "ctx", None), P("ctx", "dp"), P("ctx")
    in_specs = (whole, P("dp", "ctx"), gain, rows, rows, rows, rows, gain, rows, rows, rows, whole)
    out_specs = (whole, whole, gain, rows, rows, rows, rows, gain, rows, rows, rows)
    return jax.shard_map(
        functools.partial(layer, nd, nc),
        mesh=mesh,
        in_specs=in_specs,
        out_specs=out_specs,
        check_vma=False,
    )
```
